1024 devices in a mesh: lat: 64 (over x, y, z_hi), lon: 16 (over z_lo, core).
Axes of the slice: x: 4, y: 4, z: 32 (z_hi: 4, z_lo: 8; z = z_hi * 8 + z_lo), core: 2. Of those that a mesh axis runs over, the one named last changes fastest.
Arguments:
- query_field: bfloat16 [512, 256, 512], P('lat', 'lon'), may hold values from -6 to 6
- key_field: bfloat16 [512, 256, 512], P('lat', 'lon'), may hold values from -6 to 6
- value_field: bfloat16 [512, 256, 512], P('lat', 'lon'), may hold values from -6 to 6
- out_grad: bfloat16 [512, 256, 512], P('lat', 'lon'), may hold values from -24 to 24
- pole_reach: int32 [2, 256], replicated, may hold values from 0 to 6
Outputs:
- query_grad: bfloat16 [512, 256, 512], P('lat', 'lon')
- key_grad: bfloat16 [512, 256, 512], P('lat', 'lon')
- value_grad: bfloat16 [512, 256, 512], P('lat', 'lon')
The draws below stay inside these ranges and needn't reach their ends.
All inputs are finite; a program needn't handle non-finite values.
Results may differ from the reference program's by a relative error of at most 0.012.
The reference program's roundings to bfloat16 on the way (of `probs_half` and `grad_scores`) count: a program that leaves them out, or rounds other values in their place, can miss the bound.
Values may be sent and summed in bfloat16 or wider, within the bound.
A program may use at most 32 MiB of HBM per device.

```python
import math
import jax
import jax.numpy as jnp
from jax import lax

HEADS = 16
HEAD_DIM = 32
RADIUS = 6
BAND_ROWS = 8
SECTOR_COLS = 16
D = 512
ROWS = 512
COLS = 256
N_LAT = 64
N_LON = 16


def draw_query_field(key, part):
    field = jnp.clip(jax.random.normal(jax.random.fold_in(key, 1), (ROWS, COLS, D)), -6.0, 6.0)
    return field.astype(jnp.float32).astype(jnp.bfloat16)


def draw_key_field(key, part):
    field = jnp.clip(jax.random.normal(jax.random.fold_in(key, 2), (ROWS, COLS, D)), -6.0, 6.0)
    return field.astype(jnp.float32).astype(jnp.bfloat16)


def with_ends(entries, rng, low, high):
    dims = entries.shape
    spot = [jax.random.randint(jax.random.fold_in(rng, axis), (), 0, dims[axis]) for axis in range(len(dims))]
    entries = entries.at[tuple(spot)].set(low)
    longest = dims.index(max(dims))
    spot[longest] = (spot[longest] + 1) % dims[longest]
    return entries.at[tuple(spot)].set(high)


def block_scale(key, shape, pieces, low, top_value):
    level, own = 1.0, jax.random.fold_in(key, 6)
    for dim, shards_of in pieces:
        draws = jnp.exp(jax.random.uniform(jax.random.fold_in(own, dim), (shards_of,), jnp.float32, low / len(pieces), top_value / len(pieces)))
        level = level * jnp.repeat(draws, shape[dim] // shards_of).reshape([-1 if axis == dim else 1 for axis in range(len(shape))])
    return level


def normal_values(stream_key, dims, width, bound, pieces=(), kind=jnp.bfloat16):
    result = width * jax.random.normal(stream_key, dims, jnp.float32)
    if pieces:
        result = result * block_scale(stream_key, dims, pieces, -0.22, 0.18)
    return jnp.clip(result, -bound, bound).astype(kind)


def setup_inputs(seed: int = 0) -> dict:
    splits = jax.random.split(jax.random.key(seed), 6)
    return {
        "query_field": draw_query_field(jax.random.fold_in(splits[5], 71), 0),
        "key_field": draw_key_field(jax.random.fold_in(splits[5], 71), 0),
        "value_field": normal_values(splits[2], (ROWS, COLS, D), 1.0, 6.0, ((0, 64), (1, 16))),
        "out_grad": normal_values(splits[3], (ROWS, COLS, D), 4.0, 24.0, ((0, 64), (1, 16))),
        "pole_reach": with_ends(jax.random.randint(splits[4], (2, COLS), 0, RADIUS + 1), jax.random.fold_in(splits[4], 1), 0, RADIUS).astype(jnp.int32),
    }


def lookup_row(table_row, positions, extent):
    match = positions[:, None] == jnp.arange(extent, dtype=jnp.int32)[None, :]
    return lax.optimization_barrier(jnp.sum(jnp.where(match, table_row[None, :], 0), axis=1))

def neighbour_mask(pole_reach, lat_index, lon_index, block_rows, block_cols, total_rows, total_cols):
    local_rows = jnp.arange(block_rows, dtype=jnp.int32)
    local_cols = jnp.arange(block_cols, dtype=jnp.int32)
    outer_rows = jnp.arange(block_rows + 2 * RADIUS, dtype=jnp.int32)
    outer_cols = jnp.arange(block_cols + 2 * RADIUS, dtype=jnp.int32)
    global_rows = lat_index * block_rows + local_rows
    global_cols = lon_index * block_cols + local_cols
    padded_rows = lat_index * block_rows + outer_rows
    key_cols = jnp.remainder(lon_index * block_cols + outer_cols - RADIUS + total_cols // 2, total_cols)
    north_band = padded_rows < RADIUS
    south_band = padded_rows >= total_rows + RADIUS
    north_depth = RADIUS - 1 - padded_rows
    south_depth = padded_rows - total_rows - RADIUS
    north_key = lookup_row(pole_reach[0], key_cols, total_cols)
    south_key = lookup_row(pole_reach[1], key_cols, total_cols)
    key_valid = jnp.where(north_band[:, None], north_key[None, :] > north_depth[:, None], jnp.where(south_band[:, None], south_key[None, :] > south_depth[:, None], True))
    north_query = lookup_row(pole_reach[0], global_cols, total_cols)[None, :] > global_rows[:, None]
    south_query = lookup_row(pole_reach[1], global_cols, total_cols)[None, :] > (total_rows - 1 - global_rows)[:, None]
    row_near = (outer_rows[None, :] >= local_rows[:, None]) & (outer_rows[None, :] <= local_rows[:, None] + 2 * RADIUS)
    col_near = (outer_cols[None, :] >= local_cols[:, None]) & (outer_cols[None, :] <= local_cols[:, None] + 2 * RADIUS)
    allowed = row_near[:, None, :, None] & col_near[None, :, None, :] & key_valid[None, None, :, :]
    allowed = allowed & (jnp.logical_not(north_band)[None, None, :, None] | north_query[:, :, None, None])
    allowed = allowed & (jnp.logical_not(south_band)[None, None, :, None] | south_query[:, :, None, None])
    return allowed.reshape(block_rows * block_cols, -1)

def pad_global(field):
    half_turn = COLS // 2
    north = jnp.flip(jnp.roll(field[:RADIUS], -half_turn, axis=1), axis=0)
    south = jnp.flip(jnp.roll(field[ROWS - RADIUS:], -half_turn, axis=1), axis=0)
    tall = jnp.concatenate([north, field, south], axis=0)
    return jnp.concatenate([tall[:, COLS - RADIUS:], tall, tall[:, :RADIUS]], axis=1)

def split_heads(field):
    return field.reshape(field.shape[0], HEADS, HEAD_DIM).astype(jnp.float32)

def query_block(query_rows, key_rows, value_rows, grad_rows, allowed):
    scale = 1.0 / math.sqrt(HEAD_DIM)
    query_heads = split_heads(query_rows)
    key_heads = split_heads(key_rows)
    value_heads = split_heads(value_rows)
    grad_heads = split_heads(grad_rows)
    scores = jnp.einsum('qhd,khd->hqk', query_heads, key_heads) * scale
    masked = jnp.where(allowed[None], scores, -1e+30)
    row_max = lax.optimization_barrier(jnp.max(masked, axis=2, keepdims=True))
    row_total = lax.optimization_barrier(jnp.sum(jnp.where(allowed[None], jnp.exp(masked - row_max), 0.0), axis=2, keepdims=True))
    log_total = row_max + jnp.log(row_total)
    probs = jnp.where(allowed[None], jnp.exp(scores - log_total), 0.0)
    probs_half = probs.astype(jnp.bfloat16).astype(jnp.float32)
    attended = jnp.einsum('hqk,khd->qhd', probs_half, value_heads)
    grad_dot = lax.optimization_barrier(jnp.sum(grad_heads * attended, axis=2))
    grad_probs = jnp.einsum('qhd,khd->hqk', grad_heads, value_heads)
    grad_scores = (probs * (grad_probs - grad_dot.T[:, :, None])).astype(jnp.bfloat16).astype(jnp.float32)
    query_grad = (jnp.einsum('hqk,khd->qhd', grad_scores, key_heads) * scale).astype(jnp.bfloat16)
    return (log_total[:, :, 0].T, grad_dot, query_grad.reshape(query_rows.shape[0], -1))

def key_block(key_rows, value_rows, query_outer, grad_outer, log_outer, dot_outer, allowed):
    scale = 1.0 / math.sqrt(HEAD_DIM)
    key_heads = split_heads(key_rows)
    value_heads = split_heads(value_rows)
    query_heads = split_heads(query_outer)
    grad_heads = split_heads(grad_outer)
    scores = jnp.einsum('khd,qhd->hkq', key_heads, query_heads) * scale
    probs = jnp.where(allowed[None], jnp.exp(scores - log_outer.T[:, None, :]), 0.0)
    probs_half = probs.astype(jnp.bfloat16).astype(jnp.float32)
    value_grad = jnp.einsum('hkq,qhd->khd', probs_half, grad_heads).astype(jnp.bfloat16)
    grad_probs = jnp.einsum('khd,qhd->hkq', value_heads, grad_heads)
    grad_scores = (probs * (grad_probs - dot_outer.T[:, None, :])).astype(jnp.bfloat16).astype(jnp.float32)
    key_grad = (jnp.einsum('hkq,qhd->khd', grad_scores, query_heads) * scale).astype(jnp.bfloat16)
    return (key_grad.reshape(key_rows.shape[0], -1), value_grad.reshape(key_rows.shape[0], -1))

def to_grid(stacked):
    depth = stacked.shape[-1]
    shaped = stacked.reshape(N_LAT, N_LON, BAND_ROWS, SECTOR_COLS, depth)
    return shaped.transpose(0, 2, 1, 3, 4).reshape(ROWS, COLS, depth)

def reference(query_field, key_field, value_field, out_grad, pole_reach):
    padded_query = pad_global(query_field)
    padded_key = pad_global(key_field)
    padded_value = pad_global(value_field)
    padded_grad = pad_global(out_grad)
    outer_shape = (BAND_ROWS + 2 * RADIUS, SECTOR_COLS + 2 * RADIUS)

    def cut_outer(padded, lat_index, lon_index):
        start = (lat_index * BAND_ROWS, lon_index * SECTOR_COLS, lat_index * 0)
        piece = lax.dynamic_slice(padded, start, (outer_shape[0], outer_shape[1], padded.shape[2]))
        return piece.reshape(-1, padded.shape[2])

    def cut_local(field, lat_index, lon_index):
        start = (lat_index * BAND_ROWS, lon_index * SECTOR_COLS, lat_index * 0)
        piece = lax.dynamic_slice(field, start, (BAND_ROWS, SECTOR_COLS, field.shape[2]))
        return piece.reshape(-1, field.shape[2])

    def first_pass(block):
        lat_index = block // N_LON
        lon_index = block % N_LON
        allowed = neighbour_mask(pole_reach, lat_index, lon_index, BAND_ROWS, SECTOR_COLS, ROWS, COLS)
        return query_block(cut_local(query_field, lat_index, lon_index), cut_outer(padded_key, lat_index, lon_index), cut_outer(padded_value, lat_index, lon_index), cut_local(out_grad, lat_index, lon_index), allowed)
    blocks = jnp.arange(N_LAT * N_LON, dtype=jnp.int32)
    log_stack, dot_stack, query_stack = lax.map(first_pass, blocks)
    padded_log = pad_global(to_grid(log_stack))
    padded_dot = pad_global(to_grid(dot_stack))

    def second_pass(block):
        lat_index = block // N_LON
        lon_index = block % N_LON
        allowed = neighbour_mask(pole_reach, lat_index, lon_index, BAND_ROWS, SECTOR_COLS, ROWS, COLS)
        return key_block(cut_local(key_field, lat_index, lon_index), cut_local(value_field, lat_index, lon_index), cut_outer(padded_query, lat_index, lon_index), cut_outer(padded_grad, lat_index, lon_index), cut_outer(padded_log, lat_index, lon_index), cut_outer(padded_dot, lat_index, lon_index), allowed)
    key_stack, value_stack = lax.map(second_pass, blocks)
    return (to_grid(query_stack), to_grid(key_stack), to_grid(value_stack))
```

```python
import functools
import math

import jax
import jax.numpy as jnp
from jax import lax
from jax.experimental import pallas as pl
from jax.experimental.pallas import tpu as pltpu
from jax.sharding import PartitionSpec as P

HEAD_DIM = 32
RADIUS = 6
LANES = 128
GROUP = LANES // HEAD_DIM
EDGE = 8
MESH = pl.DeviceIdType.MESH
LOG2E = 1.4426950408889634
NEG = -1e30


def dot_nt(a, b):
    return lax.dot_general(a, b, (((1,), (1,)), ((), ())), preferred_element_type=jnp.float32)


def dot_nn(a, b):
    return lax.dot_general(a, b, (((1,), (0,)), ((), ())), preferred_element_type=jnp.float32)


def kernel(
    n_lat,
    n_lon,
    rows,
    cols,
    groups,
    q_ref,
    k_ref,
    v_ref,
    g_ref,
    reach_ref,
    dq_ref,
    dk_ref,
    dv_ref,
    field,
    stat,
    stat_own,
    bias,
    local_sem,
    lat_send,
    lat_recv,
    lon_send,
    lon_recv,
    stat_lat_send,
    stat_lat_recv,
    stat_lon_send,
    stat_lon_recv,
):
    lat, lon = lax.axis_index("lat"), lax.axis_index("lon")
    tall, wide = rows + 2 * RADIUS, cols + 2 * EDGE
    own, outer = rows * cols, tall * wide
    low = RADIUS + rows
    at_north = (n_lat - 1 - lat) // (n_lat - 1)
    at_south = lat // (n_lat - 1)
    up = (lat - 1 + at_north, (lon + at_north * (n_lon // 2)) % n_lon)
    down = (lat + 1 - at_south, (lon + at_south * (n_lon // 2)) % n_lon)
    up_slot, down_slot = 1 - at_north, at_south
    left = (lat, (lon + n_lon - 1) % n_lon)
    right = (lat, (lon + 1) % n_lon)

    sources = (k_ref, v_ref, q_ref, g_ref)

    def local_copy(g, a):
        return pltpu.make_async_copy(
            sources[a].at[:, :, pl.ds(g * LANES, LANES)],
            field.at[g, a, pl.ds(RADIUS, rows), pl.ds(EDGE, cols), :],
            local_sem.at[g, a],
        )

    for pair in range(2):
        for g in range(groups):
            for a in range(2):
                local_copy(g, 2 * pair + a).start()

    barrier = pltpu.get_barrier_semaphore()
    for device in (up, down, left, right):
        pl.semaphore_signal(barrier, inc=1, device_id=device, device_id_type=MESH)

    def lat_copy(pair, g, way):
        arrays = pl.ds(2 * pair, 2)
        slot = (up_slot, down_slot)[way]
        return pltpu.make_async_remote_copy(
            src_ref=field.at[g, arrays, pl.ds((RADIUS, rows)[way], RADIUS), pl.ds(EDGE, cols), :],
            dst_ref=field.at[g, arrays, pl.ds(slot * low, RADIUS), pl.ds(EDGE, cols), :],
            send_sem=lat_send.at[pair, g, way],
            recv_sem=lat_recv.at[pair, g, slot],
            device_id=(up, down)[way],
            device_id_type=MESH,
        )

    def lat_arrival(pair, g, slot):
        arrays = pl.ds(2 * pair, 2)
        there = field.at[g, arrays, pl.ds(slot * low, RADIUS), pl.ds(EDGE, cols), :]
        return pltpu.make_async_remote_copy(
            src_ref=there,
            dst_ref=there,
            send_sem=lat_send.at[pair, g, slot],
            recv_sem=lat_recv.at[pair, g, slot],
            device_id=up,
            device_id_type=MESH,
        )

    def lon_copy(pair, g, way):
        arrays = pl.ds(2 * pair, 2)
        return pltpu.make_async_remote_copy(
            src_ref=field.at[g, arrays, :, pl.ds((EDGE, cols)[way], EDGE), :],
            dst_ref=field.at[g, arrays, :, pl.ds((EDGE + cols, 0)[way], EDGE), :],
            send_sem=lon_send.at[pair, g, way],
            recv_sem=lon_recv.at[pair, g, way],
            device_id=(left, right)[way],
            device_id_type=MESH,
        )

    def stat_lat_copy(way):
        slot = (up_slot, down_slot)[way]
        return pltpu.make_async_remote_copy(
            src_ref=stat.at[pl.ds((RADIUS, rows)[way], RADIUS), pl.ds(EDGE, cols), :],
            dst_ref=stat.at[pl.ds(slot * low, RADIUS), pl.ds(EDGE, cols), :],
            send_sem=stat_lat_send.at[way],
            recv_sem=stat_lat_recv.at[slot],
            device_id=(up, down)[way],
            device_id_type=MESH,
        )

    def stat_lat_arrival(slot):
        there = stat.at[pl.ds(slot * low, RADIUS), pl.ds(EDGE, cols), :]
        return pltpu.make_async_remote_copy(
            src_ref=there,
            dst_ref=there,
            send_sem=stat_lat_send.at[slot],
            recv_sem=stat_lat_recv.at[slot],
            device_id=up,
            device_id_type=MESH,
        )

    def stat_lon_copy(way):
        return pltpu.make_async_remote_copy(
            src_ref=stat.at[:, pl.ds((EDGE, cols)[way], EDGE), :],
            dst_ref=stat.at[:, pl.ds((EDGE + cols, 0)[way], EDGE), :],
            send_sem=stat_lon_send.at[way],
            recv_sem=stat_lon_recv.at[way],
            device_id=(left, right)[way],
            device_id_type=MESH,
        )

    def send_lat(pair, g):
        for way in range(2):
            lat_copy(pair, g, way).start()

    pl.semaphore_wait(barrier, 4)
    for g in range(groups):
        for a in range(2):
            local_copy(g, a).wait()
        send_lat(0, g)
    for g in range(groups):
        for a in range(2, 4):
            local_copy(g, a).wait()
    send_lat(1, 0)

    total_cols = n_lon * cols
    reach = reach_ref[...].astype(jnp.float32)
    pick = lax.broadcasted_iota(jnp.int32, (16, total_cols), 0)
    table = jnp.where(
        pick == 0,
        jnp.broadcast_to(reach[0:1], (16, total_cols)),
        jnp.where(pick == 1, jnp.broadcast_to(reach[1:2], (16, total_cols)), 0.0),
    ).astype(jnp.bfloat16)
    outer_at = lax.broadcasted_iota(jnp.int32, (total_cols, outer), 1)
    outer_col = (lon * cols + outer_at % wide + (total_cols - EDGE + total_cols // 2)) % total_cols
    hit = lax.broadcasted_iota(jnp.int32, (total_cols, outer), 0) == outer_col
    key_reach = dot_nn(table, jnp.where(hit, 1.0, 0.0).astype(jnp.bfloat16))
    own_at = lax.broadcasted_iota(jnp.int32, (own, total_cols), 0)
    hit = lax.broadcasted_iota(jnp.int32, (own, total_cols), 1) == lon * cols + own_at % cols
    query_reach = dot_nt(jnp.where(hit, 1.0, 0.0).astype(jnp.bfloat16), table)
    k_at = lax.broadcasted_iota(jnp.int32, (1, outer), 1)
    k_row, k_col = k_at // wide, k_at % wide - EDGE
    k_north = (k_row < RADIUS) & (at_north == 1)
    k_south = (k_row >= low) & (at_south == 1)
    k_place = jnp.where(
        k_north, -1 - k_row, jnp.where(k_south, low + low - 1 - k_row, k_row - RADIUS)
    )
    k_depth = jnp.where(k_north, k_row, tall - 1 - k_row).astype(jnp.float32)
    k_polar = jnp.where(k_north, 1.0, jnp.where(k_south, 2.0, 0.0))
    k_ok = jnp.where(
        k_north,
        jnp.where(key_reach[0:1] > k_depth, 1.0, 0.0),
        jnp.where(k_south, jnp.where(key_reach[1:2] > k_depth, 1.0, 0.0), 1.0),
    )
    q_at = lax.broadcasted_iota(jnp.int32, (own, 1), 0)
    q_row, q_col = q_at // cols, q_at % cols
    q_north = jnp.where(query_reach[:, 0:1] > q_row.astype(jnp.float32), 1.0, 0.0)
    q_south = jnp.where(query_reach[:, 1:2] > (rows - 1 - q_row).astype(jnp.float32), 1.0, 0.0)
    near = (jnp.abs(k_place - q_row) <= RADIUS) & (jnp.abs(k_col - q_col) <= RADIUS)
    q_ok = jnp.where(k_polar == 1.0, q_north, jnp.where(k_polar == 2.0, q_south, 1.0))
    bias[...] = jnp.where(near & (q_ok * k_ok > 0.5), 0.0, NEG)

    lane = lax.broadcasted_iota(jnp.int32, (1, LANES), 1)
    in_head = [jnp.where(lane // HEAD_DIM == h, 1.0, 0.0) for h in range(GROUP)]
    in_head_half = [mask.astype(jnp.bfloat16) for mask in in_head]
    scale = 1.0 / math.sqrt(HEAD_DIM)
    to_log2 = scale * LOG2E

    def own_part(g, a):
        return field[g, a, pl.ds(RADIUS, rows), pl.ds(EDGE, cols), :].reshape(own, LANES)

    def outer_part(g, a):
        return field[g, a].reshape(outer, LANES)

    def features(g):
        return pl.ds(pl.multiple_of(g * LANES, LANES), LANES)

    stat_own[...] = jnp.zeros_like(stat_own)

    def query_step(g, carry):
        for slot in range(2):
            lat_arrival(0, g, slot).wait_recv()
        for way in range(2):
            lon_copy(0, g, way).start()
        query, grad = own_part(g, 2), own_part(g, 3)
        for way in range(2):
            lon_copy(0, g, way).wait_recv()
        key, value = outer_part(g, 0), outer_part(g, 1)
        query_grad = jnp.zeros((own, LANES), jnp.float32)
        stats = stat_own[...]
        for h in range(GROUP):
            grad_h = grad * in_head_half[h]
            logits = dot_nt(query * in_head_half[h], key) * to_log2 + bias[...]
            top = jnp.max(logits, axis=1, keepdims=True)
            weight = jnp.exp2(logits - top)
            total = jnp.sum(weight, axis=1, keepdims=True)
            probs = weight * (1.0 / total)
            attended = dot_nn(probs.astype(jnp.bfloat16), value)
            grad_dot = jnp.sum(grad_h.astype(jnp.float32) * attended, axis=1, keepdims=True)
            grad_probs = dot_nt(grad_h, value)
            grad_scores = (probs * (grad_probs - grad_dot)).astype(jnp.bfloat16)
            query_grad += dot_nn(grad_scores, key) * in_head[h]
            log_total = (top + jnp.log(total) * LOG2E) * (1.0 / to_log2)
            head = g * GROUP + h
            for part, stat_value in enumerate((log_total, grad_dot)):
                rest = -stat_value
                for piece in range(3):
                    kept = rest.astype(jnp.bfloat16).astype(jnp.float32)
                    rest = rest - kept
                    stats = jnp.where(lane == (3 * part + piece) * 16 + head, kept, stats)
        stat_own[...] = stats
        dq_ref[:, :, features(g)] = (
            (query_grad * scale).astype(jnp.bfloat16).reshape(rows, cols, LANES)
        )
        return carry

    lax.fori_loop(0, groups, query_step, 0)

    stat[pl.ds(RADIUS, rows), pl.ds(EDGE, cols), :] = (
        stat_own[...].astype(jnp.bfloat16).reshape(rows, cols, LANES)
    )
    for way in range(2):
        stat_lat_copy(way).start()
    for g in range(1, groups):
        send_lat(1, g)
    for slot in range(2):
        stat_lat_arrival(slot).wait_recv()
    for way in range(2):
        stat_lon_copy(way).start()

    def key_step(g, carry):
        for slot in range(2):
            lat_arrival(1, g, slot).wait_recv()
        for way in range(2):
            lon_copy(1, g, way).start()

        @pl.when(g == 0)
        def _():
            for way in range(2):
                stat_lon_copy(way).wait_recv()

        key, value = own_part(g, 0), own_part(g, 1)
        for way in range(2):
            lon_copy(1, g, way).wait_recv()
        query, grad = outer_part(g, 2), outer_part(g, 3)
        outer_stat = stat[...].reshape(outer, LANES)
        query_stat = jnp.concatenate([query, outer_stat], axis=1)
        grad_stat = jnp.concatenate([grad, outer_stat], axis=1)
        key_grad = jnp.zeros((own, LANES), jnp.float32)
        value_grad = jnp.zeros((own, LANES), jnp.float32)
        for h in range(GROUP):
            mine = lane % 16 == g * GROUP + h
            in_log = jnp.where(mine & (lane < 48), 1.0, 0.0).astype(jnp.bfloat16)
            in_dot = jnp.where(mine & (lane >= 48) & (lane < 96), 1.0, 0.0).astype(jnp.bfloat16)
            in_log = jnp.broadcast_to(in_log, (own, LANES))
            in_dot = jnp.broadcast_to(in_dot, (own, LANES))
            key_h = jnp.concatenate([key * in_head_half[h], in_log], axis=1)
            value_h = jnp.concatenate([value * in_head_half[h], in_dot], axis=1)
            probs = jnp.exp2(dot_nt(key_h, query_stat) * to_log2 + bias[...])
            value_grad += dot_nn(probs.astype(jnp.bfloat16), grad) * in_head[h]
            grad_scores = (probs * dot_nt(value_h, grad_stat)).astype(jnp.bfloat16)
            key_grad += dot_nn(grad_scores, query) * in_head[h]
        dk_ref[:, :, features(g)] = (
            (key_grad * scale).astype(jnp.bfloat16).reshape(rows, cols, LANES)
        )
        dv_ref[:, :, features(g)] = value_grad.astype(jnp.bfloat16).reshape(rows, cols, LANES)
        return carry

    lax.fori_loop(0, groups, key_step, 0)

    for way in range(2):
        for pair in range(2):
            for g in range(groups):
                lat_copy(pair, g, way).wait_send()
                lon_copy(pair, g, way).wait_send()
        stat_lat_copy(way).wait_send()
        stat_lon_copy(way).wait_send()


def shards(n_lat, n_lon, query_field, key_field, value_field, out_grad, pole_reach):
    rows, cols, width = query_field.shape
    groups = width // LANES
    tall, wide = rows + 2 * RADIUS, cols + 2 * EDGE
    shape = jax.ShapeDtypeStruct((rows, cols, width), jnp.bfloat16)
    dma = pltpu.SemaphoreType.DMA
    return pl.pallas_call(
        functools.partial(kernel, n_lat, n_lon, rows, cols, groups),
        out_shape=(shape, shape, shape),
        in_specs=[pl.BlockSpec(memory_space=pl.ANY)] * 4 + [pl.BlockSpec(memory_space=pltpu.VMEM)],
        out_specs=[pl.BlockSpec(memory_space=pltpu.VMEM)] * 3,
        scratch_shapes=[
            pltpu.VMEM((groups, 4, tall, wide, LANES), jnp.bfloat16),
            pltpu.VMEM((tall, wide, LANES), jnp.bfloat16),
            pltpu.VMEM((rows * cols, LANES), jnp.float32),
            pltpu.VMEM((rows * cols, tall * wide), jnp.float32),
            dma((groups, 4)),
            dma((2, groups, 2)),
            dma((2, groups, 2)),
            dma((2, groups, 2)),
            dma((2, groups, 2)),
            dma((2,)),
            dma((2,)),
            dma((2,)),
            dma((2,)),
        ],
        compiler_params=pltpu.CompilerParams(
            collective_id=0, has_side_effects=True, vmem_limit_bytes=40 << 20
        ),
    )(query_field, key_field, value_field, out_grad, pole_reach)


def solution(mesh):
    placed = P("lat", "lon", None)
    return jax.shard_map(
        functools.partial(shards, mesh.shape["lat"], mesh.shape["lon"]),
        mesh=mesh,
        in_specs=(placed, placed, placed, placed, P()),
        out_specs=(placed, placed, placed),
        check_vma=False,
    )
```

```python
import functools
import math

import jax
import jax.numpy as jnp
from jax import lax
from jax.experimental import pallas as pl
from jax.experimental.pallas import tpu as pltpu
from jax.sharding import PartitionSpec as P

HEAD_DIM = 32
RADIUS = 6
LANES = 128
GROUP = LANES // HEAD_DIM
EDGE = 8
MESH = pl.DeviceIdType.MESH
LOG2E = 1.4426950408889634
NEG = -1e30


def dot_nt(a, b):
    return lax.dot_general(a, b, (((1,), (1,)), ((), ())), preferred_element_type=jnp.float32)


def dot_nn(a, b):
    return lax.dot_general(a, b, (((1,), (0,)), ((), ())), preferred_element_type=jnp.float32)


def kernel(
    n_lat,
    n_lon,
    rows,
    cols,
    groups,
    q_ref,
    k_ref,
    v_ref,
    g_ref,
    reach_hbm,
    dq_ref,
    dk_ref,
    dv_ref,
    field,
    stat,
    stat_own,
    bias,
    reach_ref,
    reach_sem,
    local_sem,
    lat_send,
    lat_recv,
    lon_send,
    lon_recv,
    lon_own_send,
    lon_own_recv,
    relayed,
    relay_send,
    relay_recv,
    relay_on_send,
    stat_lat_send,
    stat_lat_recv,
    stat_lon_send,
    stat_lon_recv,
):
    lat, lon = lax.axis_index("lat"), lax.axis_index("lon")
    tall, wide = rows + 2 * RADIUS, cols + 2 * EDGE
    own, outer = rows * cols, tall * wide
    own_rows, halo_rows = pl.ds(0, rows), pl.ds(rows, 2 * RADIUS)
    at_north = (n_lat - 1 - lat) // (n_lat - 1)
    at_south = lat // (n_lat - 1)
    up = (lat - 1 + at_north, (lon + at_north * (n_lon // 2)) % n_lon)
    down = (lat + 1 - at_south, (lon + at_south * (n_lon // 2)) % n_lon)
    up_slot, down_slot = 1 - at_north, at_south
    left = (lat, (lon + n_lon - 1) % n_lon)
    right = (lat, (lon + 1) % n_lon)

    sources = (k_ref, v_ref, q_ref, g_ref)

    def local_copy(g, a):
        return pltpu.make_async_copy(
            sources[a].at[:, :, pl.ds(g * LANES, LANES)],
            field.at[g, a, own_rows, pl.ds(EDGE, cols), :],
            local_sem.at[g, a],
        )

    for pair in range(2):
        for g in range(groups):
            for a in range(2):
                local_copy(g, 2 * pair + a).start()

    reach_copy = pltpu.make_async_copy(reach_hbm, reach_ref, reach_sem)
    reach_copy.start()

    half_lon = n_lon // 2
    half = lon // half_lon
    north_relay, south_relay = n_lat - 4, 3
    north_source, south_source = at_north * (1 - half), at_south * half
    in_north_relay = (lat == north_relay) & (half == 0)
    in_south_relay = (lat == south_relay) & (half == 1)
    relay = (
        at_north * north_relay + at_south * south_relay,
        lon % half_lon + at_south * half_lon,
    )
    relay_ends = (
        ((0, lon), (0, (lon + half_lon) % n_lon)),
        ((n_lat - 1, lon), (n_lat - 1, (lon + half_lon) % n_lon)),
    )

    barrier = pltpu.get_barrier_semaphore()

    def greet(device):
        pl.semaphore_signal(barrier, inc=1, device_id=device, device_id_type=MESH)

    for device in (up, down, left, right):
        greet(device)

    @pl.when(at_north + at_south == 1)
    def _():
        greet(relay)

    for inside, ends in zip((in_north_relay, in_south_relay), relay_ends):

        @pl.when(inside)
        def _(ends=ends):
            for device in ends:
                greet(device)

    def relay_copy(pair, way):
        arrays = pl.ds(2 * pair, 2)
        return pltpu.make_async_remote_copy(
            src_ref=field.at[:, arrays, pl.ds((0, rows - RADIUS)[way], RADIUS), pl.ds(EDGE, cols), :],
            dst_ref=relayed.at[:, arrays],
            send_sem=relay_send.at[pair],
            recv_sem=relay_recv.at[pair],
            device_id=relay,
            device_id_type=MESH,
        )

    def relay_on(pair, g, slot):
        arrays = pl.ds(2 * pair, 2)
        return pltpu.make_async_remote_copy(
            src_ref=relayed.at[g, arrays],
            dst_ref=field.at[g, arrays, pl.ds(rows + slot * RADIUS, RADIUS), pl.ds(EDGE, cols), :],
            send_sem=relay_on_send.at[pair, g],
            recv_sem=lat_recv.at[pair, g, slot],
            device_id=relay_ends[slot][1],
            device_id_type=MESH,
        )

    def lat_copy(pair, g, way):
        arrays = pl.ds(2 * pair, 2)
        slot = (up_slot, down_slot)[way]
        return pltpu.make_async_remote_copy(
            src_ref=field.at[g, arrays, pl.ds((0, rows - RADIUS)[way], RADIUS), pl.ds(EDGE, cols), :],
            dst_ref=field.at[g, arrays, pl.ds(rows + slot * RADIUS, RADIUS), pl.ds(EDGE, cols), :],
            send_sem=lat_send.at[pair, g, way],
            recv_sem=lat_recv.at[pair, g, slot],
            device_id=(up, down)[way],
            device_id_type=MESH,
        )

    def lat_arrival(pair, g, slot):
        arrays = pl.ds(2 * pair, 2)
        there = field.at[g, arrays, pl.ds(rows + slot * RADIUS, RADIUS), pl.ds(EDGE, cols), :]
        return pltpu.make_async_remote_copy(
            src_ref=there,
            dst_ref=there,
            send_sem=lat_send.at[pair, g, slot],
            recv_sem=lat_recv.at[pair, g, slot],
            device_id=up,
            device_id_type=MESH,
        )

    def lon_copy(pair, g, way):
        arrays = pl.ds(2 * pair, 2)
        return pltpu.make_async_remote_copy(
            src_ref=field.at[g, arrays, halo_rows, pl.ds((EDGE, cols)[way], EDGE), :],
            dst_ref=field.at[g, arrays, halo_rows, pl.ds((EDGE + cols, 0)[way], EDGE), :],
            send_sem=lon_send.at[pair, g, way],
            recv_sem=lon_recv.at[pair, g, way],
            device_id=(left, right)[way],
            device_id_type=MESH,
        )

    def lon_own_copy(pair, way):
        arrays = pl.ds(2 * pair, 2)
        return pltpu.make_async_remote_copy(
            src_ref=field.at[:, arrays, own_rows, pl.ds((EDGE, cols)[way], EDGE), :],
            dst_ref=field.at[:, arrays, own_rows, pl.ds((EDGE + cols, 0)[way], EDGE), :],
            send_sem=lon_own_send.at[pair, way],
            recv_sem=lon_own_recv.at[pair, way],
            device_id=(left, right)[way],
            device_id_type=MESH,
        )

    def stat_lat_copy(way):
        slot = (up_slot, down_slot)[way]
        return pltpu.make_async_remote_copy(
            src_ref=stat.at[pl.ds((0, rows - RADIUS)[way], RADIUS), pl.ds(EDGE, cols), :],
            dst_ref=stat.at[pl.ds(rows + slot * RADIUS, RADIUS), pl.ds(EDGE, cols), :],
            send_sem=stat_lat_send.at[way],
            recv_sem=stat_lat_recv.at[slot],
            device_id=(up, down)[way],
            device_id_type=MESH,
        )

    def stat_lat_arrival(slot):
        there = stat.at[pl.ds(rows + slot * RADIUS, RADIUS), pl.ds(EDGE, cols), :]
        return pltpu.make_async_remote_copy(
            src_ref=there,
            dst_ref=there,
            send_sem=stat_lat_send.at[slot],
            recv_sem=stat_lat_recv.at[slot],
            device_id=up,
            device_id_type=MESH,
        )

    def stat_lon_copy(part, way):
        span = (own_rows, halo_rows)[part]
        return pltpu.make_async_remote_copy(
            src_ref=stat.at[span, pl.ds((EDGE, cols)[way], EDGE), :],
            dst_ref=stat.at[span, pl.ds((EDGE + cols, 0)[way], EDGE), :],
            send_sem=stat_lon_send.at[part, way],
            recv_sem=stat_lon_recv.at[part, way],
            device_id=(left, right)[way],
            device_id_type=MESH,
        )

    def each_lat(chunks, act):
        for skipped, ways in ((north_source, (1,)), (south_source, (0,)), (None, (0, 1))):
            here = north_source + south_source == 0 if skipped is None else skipped == 1

            @pl.when(here)
            def _(ways=ways):
                for pair, g in chunks:
                    for way in ways:
                        act(lat_copy(pair, g, way))

    def start(copy):
        copy.start()

    def wait_send(copy):
        copy.wait_send()

    for g in range(groups):
        for a in range(4):
            local_copy(g, a).wait()
    polar, relaying = at_north + at_south == 1, in_north_relay | in_south_relay
    for here, peers in (
        (polar, 5),
        (relaying, 6),
        (jnp.logical_not(polar | relaying), 4),
    ):

        @pl.when(here)
        def _(peers=peers):
            pl.semaphore_wait(barrier, peers)

    for way, source in enumerate((north_source, south_source)):

        @pl.when(source == 1)
        def _(way=way):
            for pair in range(2):
                relay_copy(pair, way).start()

    for way in range(2):
        lon_own_copy(0, way).start()
    ahead = groups // 2
    each_lat([(0, g) for g in range(groups)] + [(1, g) for g in range(ahead)], start)
    for way in range(2):
        lon_own_copy(1, way).start()
    reach_copy.wait()

    total_cols = n_lon * cols
    reach = reach_ref[...].astype(jnp.float32)
    pick = lax.broadcasted_iota(jnp.int32, (16, total_cols), 0)
    table = jnp.where(
        pick == 0,
        jnp.broadcast_to(reach[0:1], (16, total_cols)),
        jnp.where(pick == 1, jnp.broadcast_to(reach[1:2], (16, total_cols)), 0.0),
    ).astype(jnp.bfloat16)
    outer_at = lax.broadcasted_iota(jnp.int32, (total_cols, outer), 1)
    outer_col = (lon * cols + outer_at % wide + (total_cols - EDGE + total_cols // 2)) % total_cols
    hit = lax.broadcasted_iota(jnp.int32, (total_cols, outer), 0) == outer_col
    key_reach = dot_nn(table, jnp.where(hit, 1.0, 0.0).astype(jnp.bfloat16))
    own_at = lax.broadcasted_iota(jnp.int32, (own, total_cols), 0)
    hit = lax.broadcasted_iota(jnp.int32, (own, total_cols), 1) == lon * cols + own_at % cols
    query_reach = dot_nt(jnp.where(hit, 1.0, 0.0).astype(jnp.bfloat16), table)
    k_at = lax.broadcasted_iota(jnp.int32, (1, outer), 1)
    k_row, k_col = k_at // wide, k_at % wide - EDGE
    k_above, k_below = k_row - rows, k_row - rows - RADIUS
    k_north = (k_above >= 0) & (k_below < 0) & (at_north == 1)
    k_south = (k_below >= 0) & (at_south == 1)
    k_place = jnp.where(
        k_below >= 0,
        jnp.where(k_south, rows + RADIUS - 1 - k_below, rows + k_below),
        jnp.where(k_above >= 0, jnp.where(k_north, -1 - k_above, k_above - RADIUS), k_row),
    )
    k_depth = jnp.where(k_north, k_above, RADIUS - 1 - k_below).astype(jnp.float32)
    k_polar = jnp.where(k_north, 1.0, jnp.where(k_south, 2.0, 0.0))
    k_ok = jnp.where(
        k_north,
        jnp.where(key_reach[0:1] > k_depth, 1.0, 0.0),
        jnp.where(k_south, jnp.where(key_reach[1:2] > k_depth, 1.0, 0.0), 1.0),
    )
    q_at = lax.broadcasted_iota(jnp.int32, (own, 1), 0)
    q_row, q_col = q_at // cols, q_at % cols
    q_north = jnp.where(query_reach[:, 0:1] > q_row.astype(jnp.float32), 1.0, 0.0)
    q_south = jnp.where(query_reach[:, 1:2] > (rows - 1 - q_row).astype(jnp.float32), 1.0, 0.0)
    near = (jnp.abs(k_place - q_row) <= RADIUS) & (jnp.abs(k_col - q_col) <= RADIUS)
    q_ok = jnp.where(k_polar == 1.0, q_north, jnp.where(k_polar == 2.0, q_south, 1.0))
    bias[...] = jnp.where(near & (q_ok * k_ok > 0.5), 0.0, NEG)

    lane = lax.broadcasted_iota(jnp.int32, (1, LANES), 1)
    in_head = [jnp.where(lane // HEAD_DIM == h, 1.0, 0.0) for h in range(GROUP)]
    in_head_half = [mask.astype(jnp.bfloat16) for mask in in_head]
    scale = 1.0 / math.sqrt(HEAD_DIM)
    to_log2 = scale * LOG2E

    def own_part(g, a):
        return field[g, a, own_rows, pl.ds(EDGE, cols), :].reshape(own, LANES)

    def outer_part(g, a):
        return field[g, a].reshape(outer, LANES)

    def features(g):
        return pl.ds(pl.multiple_of(g * LANES, LANES), LANES)

    stat_own[...] = jnp.zeros_like(stat_own)

    for slot, inside in enumerate((in_north_relay, in_south_relay)):

        @pl.when(inside)
        def _(slot=slot):
            for pair in range(2):
                relay_copy(pair, slot).wait_recv()
                for g in range(groups):
                    relay_on(pair, g, slot).start()


    def pass_on(pair, g):
        for slot in range(2):
            lat_arrival(pair, g, slot).wait_recv()
        for way in range(2):
            lon_copy(pair, g, way).start()

    pass_on(0, 0)
    for way in range(2):
        lon_own_copy(0, way).wait_recv()

    def query_step(g, carry):
        @pl.when(g + 1 < groups)
        def _():
            pass_on(0, g + 1)

        query, grad = own_part(g, 2), own_part(g, 3)
        for way in range(2):
            lon_copy(0, g, way).wait_recv()
        key, value = outer_part(g, 0), outer_part(g, 1)
        query_grad = jnp.zeros((own, LANES), jnp.float32)
        stats = stat_own[...]
        for h in range(GROUP):
            grad_h = grad * in_head_half[h]
            logits = dot_nt(query * in_head_half[h], key) * to_log2 + bias[...]
            top = jnp.max(logits, axis=1, keepdims=True)
            weight = jnp.exp2(logits - top)
            total = jnp.sum(weight, axis=1, keepdims=True)
            probs = weight * (1.0 / total)
            attended = dot_nn(probs.astype(jnp.bfloat16), value)
            grad_dot = jnp.sum(grad_h.astype(jnp.float32) * attended, axis=1, keepdims=True)
            grad_probs = dot_nt(grad_h, value)
            grad_scores = (probs * (grad_probs - grad_dot)).astype(jnp.bfloat16)
            query_grad += dot_nn(grad_scores, key) * in_head[h]
            log_total = (top + jnp.log(total) * LOG2E) * (1.0 / to_log2)
            head = g * GROUP + h
            for part, stat_value in enumerate((log_total, grad_dot)):
                rest = -stat_value
                for piece in range(3):
                    kept = rest.astype(jnp.bfloat16).astype(jnp.float32)
                    rest = rest - kept
                    stats = jnp.where(lane == (3 * part + piece) * 16 + head, kept, stats)
        stat_own[...] = stats
        dq_ref[:, :, features(g)] = (
            (query_grad * scale).astype(jnp.bfloat16).reshape(rows, cols, LANES)
        )
        return carry

    lax.fori_loop(0, groups, query_step, 0)

    stat[own_rows, pl.ds(EDGE, cols), :] = (
        stat_own[...].astype(jnp.bfloat16).reshape(rows, cols, LANES)
    )
    for way in range(2):
        stat_lat_copy(way).start()
        stat_lon_copy(0, way).start()
    each_lat([(1, g) for g in range(ahead, groups)], start)
    for g in range(ahead):
        pass_on(1, g)
    for slot in range(2):
        stat_lat_arrival(slot).wait_recv()
    for way in range(2):
        stat_lon_copy(1, way).start()
    for way in range(2):
        lon_own_copy(1, way).wait_recv()

    def key_step(g, carry):
        @pl.when(g + ahead < groups)
        def _():
            pass_on(1, g + ahead)

        @pl.when(g == 0)
        def _():
            for part in range(2):
                for way in range(2):
                    stat_lon_copy(part, way).wait_recv()

        key, value = own_part(g, 0), own_part(g, 1)
        for way in range(2):
            lon_copy(1, g, way).wait_recv()
        query, grad = outer_part(g, 2), outer_part(g, 3)
        outer_stat = stat[...].reshape(outer, LANES)
        query_stat = jnp.concatenate([query, outer_stat], axis=1)
        grad_stat = jnp.concatenate([grad, outer_stat], axis=1)
        key_grad = jnp.zeros((own, LANES), jnp.float32)
        value_grad = jnp.zeros((own, LANES), jnp.float32)
        for h in range(GROUP):
            mine = lane % 16 == g * GROUP + h
            in_log = jnp.where(mine & (lane < 48), 1.0, 0.0).astype(jnp.bfloat16)
            in_dot = jnp.where(mine & (lane >= 48) & (lane < 96), 1.0, 0.0).astype(jnp.bfloat16)
            in_log = jnp.broadcast_to(in_log, (own, LANES))
            in_dot = jnp.broadcast_to(in_dot, (own, LANES))
            key_h = jnp.concatenate([key * in_head_half[h], in_log], axis=1)
            value_h = jnp.concatenate([value * in_head_half[h], in_dot], axis=1)
            probs = jnp.exp2(dot_nt(key_h, query_stat) * to_log2 + bias[...])
            value_grad += dot_nn(probs.astype(jnp.bfloat16), grad) * in_head[h]
            grad_scores = (probs * dot_nt(value_h, grad_stat)).astype(jnp.bfloat16)
            key_grad += dot_nn(grad_scores, query) * in_head[h]
        dk_ref[:, :, features(g)] = (
            (key_grad * scale).astype(jnp.bfloat16).reshape(rows, cols, LANES)
        )
        dv_ref[:, :, features(g)] = value_grad.astype(jnp.bfloat16).reshape(rows, cols, LANES)
        return carry

    lax.fori_loop(0, groups, key_step, 0)

    each_lat([(pair, g) for pair in range(2) for g in range(groups)], wait_send)
    for way, source in enumerate((north_source, south_source)):

        @pl.when(source == 1)
        def _(way=way):
            for pair in range(2):
                relay_copy(pair, way).wait_send()

    for slot, inside in enumerate((in_north_relay, in_south_relay)):

        @pl.when(inside)
        def _(slot=slot):
            for pair in range(2):
                for g in range(groups):
                    relay_on(pair, g, slot).wait_send()

    for way in range(2):
        for pair in range(2):
            for g in range(groups):
                lon_copy(pair, g, way).wait_send()
            lon_own_copy(pair, way).wait_send()
        stat_lat_copy(way).wait_send()
        for part in range(2):
            stat_lon_copy(part, way).wait_send()


def shards(n_lat, n_lon, query_field, key_field, value_field, out_grad, pole_reach):
    rows, cols, width = query_field.shape
    groups = width // LANES
    tall, wide = rows + 2 * RADIUS, cols + 2 * EDGE
    shape = jax.ShapeDtypeStruct((rows, cols, width), jnp.bfloat16)
    dma = pltpu.SemaphoreType.DMA
    return pl.pallas_call(
        functools.partial(kernel, n_lat, n_lon, rows, cols, groups),
        out_shape=(shape, shape, shape),
        in_specs=[pl.BlockSpec(memory_space=pltpu.HBM)] * 5,
        out_specs=[pl.BlockSpec(memory_space=pltpu.VMEM)] * 3,
        scratch_shapes=[
            pltpu.VMEM((groups, 4, tall, wide, LANES), jnp.bfloat16),
            pltpu.VMEM((tall, wide, LANES), jnp.bfloat16),
            pltpu.VMEM((rows * cols, LANES), jnp.float32),
            pltpu.VMEM((rows * cols, tall * wide), jnp.float32),
            pltpu.VMEM(pole_reach.shape, jnp.int32),
            dma,
            dma((groups, 4)),
            dma((2, groups, 2)),
            dma((2, groups, 2)),
            dma((2, groups, 2)),
            dma((2, groups, 2)),
            dma((2, 2)),
            dma((2, 2)),
            pltpu.VMEM((groups, 4, RADIUS, cols, LANES), jnp.bfloat16),
            dma((2,)),
            dma((2,)),
            dma((2, groups)),
            dma((2,)),
            dma((2,)),
            dma((2, 2)),
            dma((2, 2)),
        ],
        compiler_params=pltpu.CompilerParams(
            collective_id=0, has_side_effects=True, vmem_limit_bytes=60 << 20
        ),
    )(query_field, key_field, value_field, out_grad, pole_reach)


def solution(mesh):
    placed = P("lat", "lon", None)
    return jax.shard_map(
        functools.partial(shards, mesh.shape["lat"], mesh.shape["lon"]),
        mesh=mesh,
        in_specs=(placed, placed, placed, placed, P()),
        out_specs=(placed, placed, placed),
        check_vma=False,
    )
```

```python
import functools
import math

import jax
import jax.numpy as jnp
from jax import lax
from jax.experimental import pallas as pl
from jax.experimental.pallas import tpu as pltpu
from jax.sharding import PartitionSpec as P

HEAD_DIM = 32
RADIUS = 6
LANES = 128
GROUP = LANES // HEAD_DIM
EDGE = 8
MESH = pl.DeviceIdType.MESH
LOG2E = 1.4426950408889634
NEG = -1e30


def dot_nt(a, b):
    return lax.dot_general(a, b, (((1,), (1,)), ((), ())), preferred_element_type=jnp.float32)


def dot_nn(a, b):
    return lax.dot_general(a, b, (((1,), (0,)), ((), ())), preferred_element_type=jnp.float32)


def kernel(
    n_lat,
    n_lon,
    rows,
    cols,
    groups,
    q_ref,
    k_ref,
    v_ref,
    g_ref,
    reach_hbm,
    dq_hbm,
    dk_hbm,
    dv_hbm,
    field,
    dq_ref,
    dk_ref,
    dv_ref,
    out_sem,
    stat,
    stat_own,
    bias,
    reach_ref,
    reach_sem,
    local_sem,
    lat_send,
    lat_recv,
    lon_send,
    lon_recv,
    lon_own_send,
    lon_own_recv,
    relayed,
    relay_send,
    relay_recv,
    relay_on_send,
    stat_lat_send,
    stat_lat_recv,
    stat_lon_send,
    stat_lon_recv,
):
    lat, lon = lax.axis_index("lat"), lax.axis_index("lon")
    tall, wide = rows + 2 * RADIUS, cols + 2 * EDGE
    own, outer = rows * cols, tall * wide
    own_rows, halo_rows = pl.ds(0, rows), pl.ds(rows, 2 * RADIUS)
    at_north = (n_lat - 1 - lat) // (n_lat - 1)
    at_south = lat // (n_lat - 1)
    up = (lat - 1 + at_north, (lon + at_north * (n_lon // 2)) % n_lon)
    down = (lat + 1 - at_south, (lon + at_south * (n_lon // 2)) % n_lon)
    up_slot, down_slot = 1 - at_north, at_south
    left = (lat, (lon + n_lon - 1) % n_lon)
    right = (lat, (lon + 1) % n_lon)

    sources = (k_ref, v_ref, q_ref, g_ref)

    def local_copy(g, a):
        return pltpu.make_async_copy(
            sources[a].at[:, :, pl.ds(g * LANES, LANES)],
            field.at[g, a, own_rows, pl.ds(EDGE, cols), :],
            local_sem.at[g, a],
        )

    for pair in range(2):
        for g in range(groups):
            for a in range(2):
                local_copy(g, 2 * pair + a).start()

    reach_copy = pltpu.make_async_copy(reach_hbm, reach_ref, reach_sem)
    reach_copy.start()

    half_lon = n_lon // 2
    half = lon // half_lon
    north_relay, south_relay = n_lat - 4, 3
    north_source, south_source = at_north * (1 - half), at_south * half
    in_north_relay = (lat == north_relay) & (half == 0)
    in_south_relay = (lat == south_relay) & (half == 1)
    relay = (
        at_north * north_relay + at_south * south_relay,
        lon % half_lon + at_south * half_lon,
    )
    relay_ends = (
        ((0, lon), (0, (lon + half_lon) % n_lon)),
        ((n_lat - 1, lon), (n_lat - 1, (lon + half_lon) % n_lon)),
    )

    barrier = pltpu.get_barrier_semaphore()

    def greet(device):
        pl.semaphore_signal(barrier, inc=1, device_id=device, device_id_type=MESH)

    for device in (up, down, left, right):
        greet(device)

    @pl.when(at_north + at_south == 1)
    def _():
        greet(relay)

    for inside, ends in zip((in_north_relay, in_south_relay), relay_ends):

        @pl.when(inside)
        def _(ends=ends):
            for device in ends:
                greet(device)

    def relay_copy(pair, way):
        arrays = pl.ds(2 * pair, 2)
        return pltpu.make_async_remote_copy(
            src_ref=field.at[:, arrays, pl.ds((0, rows - RADIUS)[way], RADIUS), pl.ds(EDGE, cols), :],
            dst_ref=relayed.at[:, arrays],
            send_sem=relay_send.at[pair],
            recv_sem=relay_recv.at[pair],
            device_id=relay,
            device_id_type=MESH,
        )

    def relay_on(pair, g, slot):
        arrays = pl.ds(2 * pair, 2)
        return pltpu.make_async_remote_copy(
            src_ref=relayed.at[g, arrays],
            dst_ref=field.at[g, arrays, pl.ds(rows + slot * RADIUS, RADIUS), pl.ds(EDGE, cols), :],
            send_sem=relay_on_send.at[pair, g],
            recv_sem=lat_recv.at[pair, g, slot],
            device_id=relay_ends[slot][1],
            device_id_type=MESH,
        )

    def lat_copy(pair, g, way):
        arrays = pl.ds(2 * pair, 2)
        slot = (up_slot, down_slot)[way]
        return pltpu.make_async_remote_copy(
            src_ref=field.at[g, arrays, pl.ds((0, rows - RADIUS)[way], RADIUS), pl.ds(EDGE, cols), :],
            dst_ref=field.at[g, arrays, pl.ds(rows + slot * RADIUS, RADIUS), pl.ds(EDGE, cols), :],
            send_sem=lat_send.at[pair, g, way],
            recv_sem=lat_recv.at[pair, g, slot],
            device_id=(up, down)[way],
            device_id_type=MESH,
        )

    def lat_arrival(pair, g, slot):
        arrays = pl.ds(2 * pair, 2)
        there = field.at[g, arrays, pl.ds(rows + slot * RADIUS, RADIUS), pl.ds(EDGE, cols), :]
        return pltpu.make_async_remote_copy(
            src_ref=there,
            dst_ref=there,
            send_sem=lat_send.at[pair, g, slot],
            recv_sem=lat_recv.at[pair, g, slot],
            device_id=up,
            device_id_type=MESH,
        )

    def lon_copy(pair, g, way):
        arrays = pl.ds(2 * pair, 2)
        return pltpu.make_async_remote_copy(
            src_ref=field.at[g, arrays, halo_rows, pl.ds((EDGE, cols)[way], EDGE), :],
            dst_ref=field.at[g, arrays, halo_rows, pl.ds((EDGE + cols, 0)[way], EDGE), :],
            send_sem=lon_send.at[pair, g, way],
            recv_sem=lon_recv.at[pair, g, way],
            device_id=(left, right)[way],
            device_id_type=MESH,
        )

    def lon_own_copy(pair, way):
        arrays = pl.ds(2 * pair, 2)
        return pltpu.make_async_remote_copy(
            src_ref=field.at[:, arrays, own_rows, pl.ds((EDGE, cols)[way], EDGE), :],
            dst_ref=field.at[:, arrays, own_rows, pl.ds((EDGE + cols, 0)[way], EDGE), :],
            send_sem=lon_own_send.at[pair, way],
            recv_sem=lon_own_recv.at[pair, way],
            device_id=(left, right)[way],
            device_id_type=MESH,
        )

    def stat_lat_copy(way):
        slot = (up_slot, down_slot)[way]
        return pltpu.make_async_remote_copy(
            src_ref=stat.at[pl.ds((0, rows - RADIUS)[way], RADIUS), pl.ds(EDGE, cols), :],
            dst_ref=stat.at[pl.ds(rows + slot * RADIUS, RADIUS), pl.ds(EDGE, cols), :],
            send_sem=stat_lat_send.at[way],
            recv_sem=stat_lat_recv.at[slot],
            device_id=(up, down)[way],
            device_id_type=MESH,
        )

    def stat_lat_arrival(slot):
        there = stat.at[pl.ds(rows + slot * RADIUS, RADIUS), pl.ds(EDGE, cols), :]
        return pltpu.make_async_remote_copy(
            src_ref=there,
            dst_ref=there,
            send_sem=stat_lat_send.at[slot],
            recv_sem=stat_lat_recv.at[slot],
            device_id=up,
            device_id_type=MESH,
        )

    def stat_lon_copy(part, way):
        span = (own_rows, halo_rows)[part]
        return pltpu.make_async_remote_copy(
            src_ref=stat.at[span, pl.ds((EDGE, cols)[way], EDGE), :],
            dst_ref=stat.at[span, pl.ds((EDGE + cols, 0)[way], EDGE), :],
            send_sem=stat_lon_send.at[part, way],
            recv_sem=stat_lon_recv.at[part, way],
            device_id=(left, right)[way],
            device_id_type=MESH,
        )

    def each_lat(chunks, act):
        for skipped, ways in ((north_source, (1,)), (south_source, (0,)), (None, (0, 1))):
            here = north_source + south_source == 0 if skipped is None else skipped == 1

            @pl.when(here)
            def _(ways=ways):
                for pair, g in chunks:
                    for way in ways:
                        act(lat_copy(pair, g, way))

    def start(copy):
        copy.start()

    def wait_send(copy):
        copy.wait_send()

    for g in range(groups):
        for a in range(4):
            local_copy(g, a).wait()
    polar, relaying = at_north + at_south == 1, in_north_relay | in_south_relay
    for here, peers in (
        (polar, 5),
        (relaying, 6),
        (jnp.logical_not(polar | relaying), 4),
    ):

        @pl.when(here)
        def _(peers=peers):
            pl.semaphore_wait(barrier, peers)

    for way, source in enumerate((north_source, south_source)):

        @pl.when(source == 1)
        def _(way=way):
            for pair in range(2):
                relay_copy(pair, way).start()

    for way in range(2):
        lon_own_copy(0, way).start()
    each_lat([(0, g) for g in range(groups)], start)
    for way in range(2):
        lon_own_copy(1, way).start()
    reach_copy.wait()

    total_cols = n_lon * cols
    reach = reach_ref[...].astype(jnp.float32)
    pick = lax.broadcasted_iota(jnp.int32, (16, total_cols), 0)
    table = jnp.where(
        pick == 0,
        jnp.broadcast_to(reach[0:1], (16, total_cols)),
        jnp.where(pick == 1, jnp.broadcast_to(reach[1:2], (16, total_cols)), 0.0),
    ).astype(jnp.bfloat16)
    outer_at = lax.broadcasted_iota(jnp.int32, (total_cols, outer), 1)
    outer_col = (lon * cols + outer_at % wide + (total_cols - EDGE + total_cols // 2)) % total_cols
    hit = lax.broadcasted_iota(jnp.int32, (total_cols, outer), 0) == outer_col
    key_reach = dot_nn(table, jnp.where(hit, 1.0, 0.0).astype(jnp.bfloat16))
    own_at = lax.broadcasted_iota(jnp.int32, (own, total_cols), 0)
    hit = lax.broadcasted_iota(jnp.int32, (own, total_cols), 1) == lon * cols + own_at % cols
    query_reach = dot_nt(jnp.where(hit, 1.0, 0.0).astype(jnp.bfloat16), table)
    k_at = lax.broadcasted_iota(jnp.int32, (1, outer), 1)
    k_row, k_col = k_at // wide, k_at % wide - EDGE
    k_above, k_below = k_row - rows, k_row - rows - RADIUS
    k_north = (k_above >= 0) & (k_below < 0) & (at_north == 1)
    k_south = (k_below >= 0) & (at_south == 1)
    k_place = jnp.where(
        k_below >= 0,
        jnp.where(k_south, rows + RADIUS - 1 - k_below, rows + k_below),
        jnp.where(k_above >= 0, jnp.where(k_north, -1 - k_above, k_above - RADIUS), k_row),
    )
    k_depth = jnp.where(k_north, k_above, RADIUS - 1 - k_below).astype(jnp.float32)
    k_polar = jnp.where(k_north, 1.0, jnp.where(k_south, 2.0, 0.0))
    k_ok = jnp.where(
        k_north,
        jnp.where(key_reach[0:1] > k_depth, 1.0, 0.0),
        jnp.where(k_south, jnp.where(key_reach[1:2] > k_depth, 1.0, 0.0), 1.0),
    )
    q_at = lax.broadcasted_iota(jnp.int32, (own, 1), 0)
    q_row, q_col = q_at // cols, q_at % cols
    q_north = jnp.where(query_reach[:, 0:1] > q_row.astype(jnp.float32), 1.0, 0.0)
    q_south = jnp.where(query_reach[:, 1:2] > (rows - 1 - q_row).astype(jnp.float32), 1.0, 0.0)
    near = (jnp.abs(k_place - q_row) <= RADIUS) & (jnp.abs(k_col - q_col) <= RADIUS)
    q_ok = jnp.where(k_polar == 1.0, q_north, jnp.where(k_polar == 2.0, q_south, 1.0))
    bias[...] = jnp.where(near & (q_ok * k_ok > 0.5), 0.0, NEG)

    lane = lax.broadcasted_iota(jnp.int32, (1, LANES), 1)
    in_head = [jnp.where(lane // HEAD_DIM == h, 1.0, 0.0) for h in range(GROUP)]
    in_head_half = [mask.astype(jnp.bfloat16) for mask in in_head]
    scale = 1.0 / math.sqrt(HEAD_DIM)
    to_log2 = scale * LOG2E

    def own_part(g, a):
        return field[g, a, own_rows, pl.ds(EDGE, cols), :].reshape(own, LANES)

    def outer_part(g, a):
        return field[g, a].reshape(outer, LANES)

    def features(g):
        return pl.ds(pl.multiple_of(g * LANES, LANES), LANES)

    results = ((dq_ref, dq_hbm), (dk_ref, dk_hbm), (dv_ref, dv_hbm))

    def out_copy(g, which):
        held, result = results[which]
        return pltpu.make_async_copy(
            held.at[g], result.at[:, :, features(g)], out_sem.at[which, g]
        )

    stat_own[...] = jnp.zeros_like(stat_own)

    for slot, inside in enumerate((in_north_relay, in_south_relay)):

        @pl.when(inside)
        def _(slot=slot):
            for pair in range(2):
                relay_copy(pair, slot).wait_recv()
                for g in range(groups):
                    relay_on(pair, g, slot).start()


    def pass_on(pair, g):
        for slot in range(2):
            lat_arrival(pair, g, slot).wait_recv()
        for way in range(2):
            lon_copy(pair, g, way).start()

    pass_on(0, 0)
    for way in range(2):
        lon_own_copy(0, way).wait_recv()

    def query_step(g, carry):
        @pl.when(g + 1 < groups)
        def _():
            pass_on(0, g + 1)

        for c in range(groups - 1):

            @pl.when(g == c)
            def _(c=c):
                each_lat([(1, c)], start)

        query, grad = own_part(g, 2), own_part(g, 3)
        for way in range(2):
            lon_copy(0, g, way).wait_recv()
        key, value = outer_part(g, 0), outer_part(g, 1)
        query_grad = jnp.zeros((own, LANES), jnp.float32)
        stats = stat_own[...]
        for h in range(GROUP):
            grad_h = grad * in_head_half[h]
            logits = dot_nt(query * in_head_half[h], key) * to_log2 + bias[...]
            top = jnp.max(logits, axis=1, keepdims=True)
            weight = jnp.exp2(logits - top)
            total = jnp.sum(weight, axis=1, keepdims=True)
            probs = weight * (1.0 / total)
            attended = dot_nn(probs.astype(jnp.bfloat16), value)
            grad_dot = jnp.sum(grad_h.astype(jnp.float32) * attended, axis=1, keepdims=True)
            grad_probs = dot_nt(grad_h, value)
            grad_scores = (probs * (grad_probs - grad_dot)).astype(jnp.bfloat16)
            query_grad += dot_nn(grad_scores, key) * in_head[h]
            log_total = (top + jnp.log(total) * LOG2E) * (1.0 / to_log2)
            head = g * GROUP + h
            for part, stat_value in enumerate((log_total, grad_dot)):
                rest = -stat_value
                for piece in range(3):
                    kept = rest.astype(jnp.bfloat16).astype(jnp.float32)
                    rest = rest - kept
                    stats = jnp.where(lane == (3 * part + piece) * 16 + head, kept, stats)
        stat_own[...] = stats
        dq_ref[g] = (query_grad * scale).astype(jnp.bfloat16).reshape(rows, cols, LANES)
        out_copy(g, 0).start()
        return carry

    lax.fori_loop(0, groups, query_step, 0)

    stat[own_rows, pl.ds(EDGE, cols), :] = (
        stat_own[...].astype(jnp.bfloat16).reshape(rows, cols, LANES)
    )
    for way in range(2):
        stat_lat_copy(way).start()
        stat_lon_copy(0, way).start()
    each_lat([(1, groups - 1)], start)
    ahead = groups // 2
    for g in range(ahead):
        pass_on(1, g)
    for slot in range(2):
        stat_lat_arrival(slot).wait_recv()
    for way in range(2):
        stat_lon_copy(1, way).start()
    for way in range(2):
        lon_own_copy(1, way).wait_recv()

    def key_step(g, carry):
        @pl.when(g + ahead < groups)
        def _():
            pass_on(1, g + ahead)

        @pl.when(g == 0)
        def _():
            for part in range(2):
                for way in range(2):
                    stat_lon_copy(part, way).wait_recv()

        key, value = own_part(g, 0), own_part(g, 1)
        for way in range(2):
            lon_copy(1, g, way).wait_recv()
        query, grad = outer_part(g, 2), outer_part(g, 3)
        outer_stat = stat[...].reshape(outer, LANES)
        query_stat = jnp.concatenate([query, outer_stat], axis=1)
        grad_stat = jnp.concatenate([grad, outer_stat], axis=1)
        key_grad = jnp.zeros((own, LANES), jnp.float32)
        value_grad = jnp.zeros((own, LANES), jnp.float32)
        for h in range(GROUP):
            mine = lane % 16 == g * GROUP + h
            in_log = jnp.where(mine & (lane < 48), 1.0, 0.0).astype(jnp.bfloat16)
            in_dot = jnp.where(mine & (lane >= 48) & (lane < 96), 1.0, 0.0).astype(jnp.bfloat16)
            in_log = jnp.broadcast_to(in_log, (own, LANES))
            in_dot = jnp.broadcast_to(in_dot, (own, LANES))
            key_h = jnp.concatenate([key * in_head_half[h], in_log], axis=1)
            value_h = jnp.concatenate([value * in_head_half[h], in_dot], axis=1)
            probs = jnp.exp2(dot_nt(key_h, query_stat) * to_log2 + bias[...])
            value_grad += dot_nn(probs.astype(jnp.bfloat16), grad) * in_head[h]
            grad_scores = (probs * dot_nt(value_h, grad_stat)).astype(jnp.bfloat16)
            key_grad += dot_nn(grad_scores, query) * in_head[h]
        dk_ref[g] = (key_grad * scale).astype(jnp.bfloat16).reshape(rows, cols, LANES)
        out_copy(g, 1).start()
        dv_ref[g] = value_grad.astype(jnp.bfloat16).reshape(rows, cols, LANES)
        out_copy(g, 2).start()
        return carry

    lax.fori_loop(0, groups, key_step, 0)

    each_lat([(pair, g) for pair in range(2) for g in range(groups)], wait_send)
    for g in range(groups):
        for which in range(3):
            out_copy(g, which).wait()
    for way, source in enumerate((north_source, south_source)):

        @pl.when(source == 1)
        def _(way=way):
            for pair in range(2):
                relay_copy(pair, way).wait_send()

    for slot, inside in enumerate((in_north_relay, in_south_relay)):

        @pl.when(inside)
        def _(slot=slot):
            for pair in range(2):
                for g in range(groups):
                    relay_on(pair, g, slot).wait_send()

    for way in range(2):
        for pair in range(2):
            for g in range(groups):
                lon_copy(pair, g, way).wait_send()
            lon_own_copy(pair, way).wait_send()
        stat_lat_copy(way).wait_send()
        for part in range(2):
            stat_lon_copy(part, way).wait_send()


def copy_kernel(a, b, c, a_out, b_out, c_out, sem):
    pairs = ((a, a_out), (b, b_out), (c, c_out))
    copies = [pltpu.make_async_copy(x, y, sem.at[i]) for i, (x, y) in enumerate(pairs)]
    for copy in copies:
        copy.start()
    for copy in copies:
        copy.wait()


def shards(n_lat, n_lon, query_field, key_field, value_field, out_grad, pole_reach):
    rows, cols, width = query_field.shape
    groups = width // LANES
    tall, wide = rows + 2 * RADIUS, cols + 2 * EDGE
    shape = jax.ShapeDtypeStruct((rows, cols, width), jnp.bfloat16)
    dma = pltpu.SemaphoreType.DMA
    results = pl.pallas_call(
        functools.partial(kernel, n_lat, n_lon, rows, cols, groups),
        out_shape=(shape, shape, shape),
        in_specs=[pl.BlockSpec(memory_space=pltpu.HBM)] * 5,
        out_specs=[pl.BlockSpec(memory_space=pltpu.HBM)] * 3,
        scratch_shapes=[
            pltpu.VMEM((groups, 4, tall, wide, LANES), jnp.bfloat16),
            pltpu.VMEM((groups, rows, cols, LANES), jnp.bfloat16),
            pltpu.VMEM((groups, rows, cols, LANES), jnp.bfloat16),
            pltpu.VMEM((groups, rows, cols, LANES), jnp.bfloat16),
            dma((3, groups)),
            pltpu.VMEM((tall, wide, LANES), jnp.bfloat16),
            pltpu.VMEM((rows * cols, LANES), jnp.float32),
            pltpu.VMEM((rows * cols, tall * wide), jnp.float32),
            pltpu.VMEM(pole_reach.shape, jnp.int32),
            dma,
            dma((groups, 4)),
            dma((2, groups, 2)),
            dma((2, groups, 2)),
            dma((2, groups, 2)),
            dma((2, groups, 2)),
            dma((2, 2)),
            dma((2, 2)),
            pltpu.VMEM((groups, 4, RADIUS, cols, LANES), jnp.bfloat16),
            dma((2,)),
            dma((2,)),
            dma((2, groups)),
            dma((2,)),
            dma((2,)),
            dma((2, 2)),
            dma((2, 2)),
        ],
        compiler_params=pltpu.CompilerParams(
            collective_id=0, has_side_effects=True, vmem_limit_bytes=60 << 20
        ),
    )(query_field, key_field, value_field, out_grad, pole_reach)
    return pl.pallas_call(
        copy_kernel,
        out_shape=(shape, shape, shape),
        in_specs=[pl.BlockSpec(memory_space=pltpu.HBM)] * 3,
        out_specs=[pl.BlockSpec(memory_space=pltpu.HBM)] * 3,
        scratch_shapes=[dma((3,))],
        compiler_params=pltpu.CompilerParams(vmem_limit_bytes=60 << 20),
    )(*results)


def solution(mesh):
    placed = P("lat", "lon", None)
    return jax.shard_map(
        functools.partial(shards, mesh.shape["lat"], mesh.shape["lon"]),
        mesh=mesh,
        in_specs=(placed, placed, placed, placed, P()),
        out_specs=(placed, placed, placed),
        check_vma=False,
    )
```

```python
import functools
import math

import jax
import jax.numpy as jnp
from jax import lax
from jax.experimental import pallas as pl
from jax.experimental.pallas import tpu as pltpu
from jax.sharding import PartitionSpec as P

HEAD_DIM = 32
RADIUS = 6
LANES = 128
GROUP = LANES // HEAD_DIM
EDGE = 8
MESH = pl.DeviceIdType.MESH
LOG2E = 1.4426950408889634
NEG = -1e30


def dot_nt(a, b):
    return lax.dot_general(a, b, (((1,), (1,)), ((), ())), preferred_element_type=jnp.float32)


def dot_nn(a, b):
    return lax.dot_general(a, b, (((1,), (0,)), ((), ())), preferred_element_type=jnp.float32)


def kernel(
    n_lat,
    n_lon,
    rows,
    cols,
    groups,
    q_ref,
    k_ref,
    v_ref,
    g_ref,
    reach_hbm,
    dq_hbm,
    dk_hbm,
    dv_hbm,
    field,
    dq_ref,
    dk_ref,
    dv_ref,
    out_sem,
    stat,
    stat_own,
    bias,
    reach_ref,
    reach_sem,
    local_sem,
    lat_send,
    lat_recv,
    lon_send,
    lon_recv,
    lon_own_send,
    lon_own_recv,
    relayed,
    relay_send,
    relay_recv,
    relay_on_send,
    stat_lat_send,
    stat_lat_recv,
    stat_lon_send,
    stat_lon_recv,
):
    lat, lon = lax.axis_index("lat"), lax.axis_index("lon")
    tall, wide = rows + 2 * RADIUS, cols + 2 * EDGE
    own, outer = rows * cols, tall * wide
    own_rows, halo_rows = pl.ds(0, rows), pl.ds(rows, 2 * RADIUS)
    at_north = (n_lat - 1 - lat) // (n_lat - 1)
    at_south = lat // (n_lat - 1)
    up = (lat - 1 + at_north, (lon + at_north * (n_lon // 2)) % n_lon)
    down = (lat + 1 - at_south, (lon + at_south * (n_lon // 2)) % n_lon)
    up_slot, down_slot = 1 - at_north, at_south
    left = (lat, (lon + n_lon - 1) % n_lon)
    right = (lat, (lon + 1) % n_lon)

    sources = (k_ref, v_ref, q_ref, g_ref)

    def local_copy(g, a):
        return pltpu.make_async_copy(
            sources[a].at[:, :, pl.ds(g * LANES, LANES)],
            field.at[g, a, own_rows, pl.ds(EDGE, cols), :],
            local_sem.at[g, a],
        )

    for pair in range(2):
        for g in range(groups):
            for a in range(2):
                local_copy(g, 2 * pair + a).start()

    reach_copy = pltpu.make_async_copy(reach_hbm, reach_ref, reach_sem)
    reach_copy.start()

    half_lon = n_lon // 2
    half = lon // half_lon
    north_relay, south_relay = n_lat - 4, 3
    north_source, south_source = at_north * (1 - half), at_south * half
    in_north_relay = (lat == north_relay) & (half == 0)
    in_south_relay = (lat == south_relay) & (half == 1)
    relay = (
        at_north * north_relay + at_south * south_relay,
        lon % half_lon + at_south * half_lon,
    )
    relay_ends = (
        ((0, lon), (0, (lon + half_lon) % n_lon)),
        ((n_lat - 1, lon), (n_lat - 1, (lon + half_lon) % n_lon)),
    )

    for edge in (pl.ds(0, EDGE), pl.ds(EDGE + cols, EDGE)):
        field[:, :, :, edge, :] = jnp.zeros((groups, 4, tall, EDGE, LANES), jnp.bfloat16)
        stat[:, edge, :] = jnp.zeros((tall, EDGE, LANES), jnp.bfloat16)

    barrier = pltpu.get_barrier_semaphore()

    def greet(device):
        pl.semaphore_signal(barrier, inc=1, device_id=device, device_id_type=MESH)

    for device in (up, down, left, right):
        greet(device)

    @pl.when(at_north + at_south == 1)
    def _():
        greet(relay)

    for inside, ends in zip((in_north_relay, in_south_relay), relay_ends):

        @pl.when(inside)
        def _(ends=ends):
            for device in ends:
                greet(device)

    def relay_copy(pair, way):
        arrays = pl.ds(2 * pair, 2)
        return pltpu.make_async_remote_copy(
            src_ref=field.at[:, arrays, pl.ds((0, rows - RADIUS)[way], RADIUS), pl.ds(EDGE, cols), :],
            dst_ref=relayed.at[:, arrays],
            send_sem=relay_send.at[pair],
            recv_sem=relay_recv.at[pair],
            device_id=relay,
            device_id_type=MESH,
        )

    def relay_on(pair, g, slot):
        arrays = pl.ds(2 * pair, 2)
        return pltpu.make_async_remote_copy(
            src_ref=relayed.at[g, arrays],
            dst_ref=field.at[g, arrays, pl.ds(rows + slot * RADIUS, RADIUS), pl.ds(EDGE, cols), :],
            send_sem=relay_on_send.at[pair, g],
            recv_sem=lat_recv.at[pair, g, slot],
            device_id=relay_ends[slot][1],
            device_id_type=MESH,
        )

    def lat_copy(pair, g, way):
        arrays = pl.ds(2 * pair, 2)
        slot = (up_slot, down_slot)[way]
        return pltpu.make_async_remote_copy(
            src_ref=field.at[g, arrays, pl.ds((0, rows - RADIUS)[way], RADIUS), pl.ds(EDGE, cols), :],
            dst_ref=field.at[g, arrays, pl.ds(rows + slot * RADIUS, RADIUS), pl.ds(EDGE, cols), :],
            send_sem=lat_send.at[pair, g, way],
            recv_sem=lat_recv.at[pair, g, slot],
            device_id=(up, down)[way],
            device_id_type=MESH,
        )

    def lat_arrival(pair, g, slot):
        arrays = pl.ds(2 * pair, 2)
        there = field.at[g, arrays, pl.ds(rows + slot * RADIUS, RADIUS), pl.ds(EDGE, cols), :]
        return pltpu.make_async_remote_copy(
            src_ref=there,
            dst_ref=there,
            send_sem=lat_send.at[pair, g, slot],
            recv_sem=lat_recv.at[pair, g, slot],
            device_id=up,
            device_id_type=MESH,
        )

    def lon_copy(pair, g, way):
        arrays = pl.ds(2 * pair, 2)
        return pltpu.make_async_remote_copy(
            src_ref=field.at[g, arrays, halo_rows, pl.ds((EDGE, EDGE + cols - RADIUS)[way], RADIUS), :],
            dst_ref=field.at[g, arrays, halo_rows, pl.ds((EDGE + cols, EDGE - RADIUS)[way], RADIUS), :],
            send_sem=lon_send.at[pair, g, way],
            recv_sem=lon_recv.at[pair, g, way],
            device_id=(left, right)[way],
            device_id_type=MESH,
        )

    def lon_own_copy(pair, way):
        arrays = pl.ds(2 * pair, 2)
        return pltpu.make_async_remote_copy(
            src_ref=field.at[:, arrays, own_rows, pl.ds((EDGE, EDGE + cols - RADIUS)[way], RADIUS), :],
            dst_ref=field.at[:, arrays, own_rows, pl.ds((EDGE + cols, EDGE - RADIUS)[way], RADIUS), :],
            send_sem=lon_own_send.at[pair, way],
            recv_sem=lon_own_recv.at[pair, way],
            device_id=(left, right)[way],
            device_id_type=MESH,
        )

    def stat_lat_copy(way):
        slot = (up_slot, down_slot)[way]
        return pltpu.make_async_remote_copy(
            src_ref=stat.at[pl.ds((0, rows - RADIUS)[way], RADIUS), pl.ds(EDGE, cols), :],
            dst_ref=stat.at[pl.ds(rows + slot * RADIUS, RADIUS), pl.ds(EDGE, cols), :],
            send_sem=stat_lat_send.at[way],
            recv_sem=stat_lat_recv.at[slot],
            device_id=(up, down)[way],
            device_id_type=MESH,
        )

    def stat_lat_arrival(slot):
        there = stat.at[pl.ds(rows + slot * RADIUS, RADIUS), pl.ds(EDGE, cols), :]
        return pltpu.make_async_remote_copy(
            src_ref=there,
            dst_ref=there,
            send_sem=stat_lat_send.at[slot],
            recv_sem=stat_lat_recv.at[slot],
            device_id=up,
            device_id_type=MESH,
        )

    def stat_lon_copy(part, way):
        span = (own_rows, halo_rows)[part]
        return pltpu.make_async_remote_copy(
            src_ref=stat.at[span, pl.ds((EDGE, EDGE + cols - RADIUS)[way], RADIUS), :],
            dst_ref=stat.at[span, pl.ds((EDGE + cols, EDGE - RADIUS)[way], RADIUS), :],
            send_sem=stat_lon_send.at[part, way],
            recv_sem=stat_lon_recv.at[part, way],
            device_id=(left, right)[way],
            device_id_type=MESH,
        )

    def each_lat(chunks, act):
        for skipped, ways in ((north_source, (1,)), (south_source, (0,)), (None, (0, 1))):
            here = north_source + south_source == 0 if skipped is None else skipped == 1

            @pl.when(here)
            def _(ways=ways):
                for pair, g in chunks:
                    for way in ways:
                        act(lat_copy(pair, g, way))

    def start(copy):
        copy.start()

    def wait_send(copy):
        copy.wait_send()

    for g in range(groups):
        for a in range(4):
            local_copy(g, a).wait()
    polar, relaying = at_north + at_south == 1, in_north_relay | in_south_relay
    for here, peers in (
        (polar, 5),
        (relaying, 6),
        (jnp.logical_not(polar | relaying), 4),
    ):

        @pl.when(here)
        def _(peers=peers):
            pl.semaphore_wait(barrier, peers)

    for way, source in enumerate((north_source, south_source)):

        @pl.when(source == 1)
        def _(way=way):
            for pair in range(2):
                relay_copy(pair, way).start()

    for way in range(2):
        lon_own_copy(0, way).start()
    each_lat([(0, g) for g in range(groups)], start)
    for way in range(2):
        lon_own_copy(1, way).start()
    reach_copy.wait()

    total_cols = n_lon * cols
    reach = reach_ref[...].astype(jnp.float32)
    pick = lax.broadcasted_iota(jnp.int32, (16, total_cols), 0)
    table = jnp.where(
        pick == 0,
        jnp.broadcast_to(reach[0:1], (16, total_cols)),
        jnp.where(pick == 1, jnp.broadcast_to(reach[1:2], (16, total_cols)), 0.0),
    ).astype(jnp.bfloat16)
    outer_at = lax.broadcasted_iota(jnp.int32, (total_cols, outer), 1)
    outer_col = (lon * cols + outer_at % wide + (total_cols - EDGE + total_cols // 2)) % total_cols
    hit = lax.broadcasted_iota(jnp.int32, (total_cols, outer), 0) == outer_col
    key_reach = dot_nn(table, jnp.where(hit, 1.0, 0.0).astype(jnp.bfloat16))
    own_at = lax.broadcasted_iota(jnp.int32, (own, total_cols), 0)
    hit = lax.broadcasted_iota(jnp.int32, (own, total_cols), 1) == lon * cols + own_at % cols
    query_reach = dot_nt(jnp.where(hit, 1.0, 0.0).astype(jnp.bfloat16), table)
    k_at = lax.broadcasted_iota(jnp.int32, (1, outer), 1)
    k_row, k_col = k_at // wide, k_at % wide - EDGE
    k_above, k_below = k_row - rows, k_row - rows - RADIUS
    k_north = (k_above >= 0) & (k_below < 0) & (at_north == 1)
    k_south = (k_below >= 0) & (at_south == 1)
    k_place = jnp.where(
        k_below >= 0,
        jnp.where(k_south, rows + RADIUS - 1 - k_below, rows + k_below),
        jnp.where(k_above >= 0, jnp.where(k_north, -1 - k_above, k_above - RADIUS), k_row),
    )
    k_depth = jnp.where(k_north, k_above, RADIUS - 1 - k_below).astype(jnp.float32)
    k_polar = jnp.where(k_north, 1.0, jnp.where(k_south, 2.0, 0.0))
    k_ok = jnp.where(
        k_north,
        jnp.where(key_reach[0:1] > k_depth, 1.0, 0.0),
        jnp.where(k_south, jnp.where(key_reach[1:2] > k_depth, 1.0, 0.0), 1.0),
    )
    q_at = lax.broadcasted_iota(jnp.int32, (own, 1), 0)
    q_row, q_col = q_at // cols, q_at % cols
    q_north = jnp.where(query_reach[:, 0:1] > q_row.astype(jnp.float32), 1.0, 0.0)
    q_south = jnp.where(query_reach[:, 1:2] > (rows - 1 - q_row).astype(jnp.float32), 1.0, 0.0)
    near = (jnp.abs(k_place - q_row) <= RADIUS) & (jnp.abs(k_col - q_col) <= RADIUS)
    q_ok = jnp.where(k_polar == 1.0, q_north, jnp.where(k_polar == 2.0, q_south, 1.0))
    bias[...] = jnp.where(near & (q_ok * k_ok > 0.5), 0.0, NEG)

    lane = lax.broadcasted_iota(jnp.int32, (1, LANES), 1)
    in_head = [jnp.where(lane // HEAD_DIM == h, 1.0, 0.0) for h in range(GROUP)]
    in_head_half = [mask.astype(jnp.bfloat16) for mask in in_head]
    scale = 1.0 / math.sqrt(HEAD_DIM)
    to_log2 = scale * LOG2E

    def own_part(g, a):
        return field[g, a, own_rows, pl.ds(EDGE, cols), :].reshape(own, LANES)

    def outer_part(g, a):
        return field[g, a].reshape(outer, LANES)

    def features(g):
        return pl.ds(pl.multiple_of(g * LANES, LANES), LANES)

    results = ((dq_ref, dq_hbm), (dk_ref, dk_hbm), (dv_ref, dv_hbm))

    def out_copy(g, which):
        held, result = results[which]
        return pltpu.make_async_copy(
            held.at[g], result.at[:, :, features(g)], out_sem.at[which, g]
        )

    stat_own[...] = jnp.zeros_like(stat_own)

    for slot, inside in enumerate((in_north_relay, in_south_relay)):

        @pl.when(inside)
        def _(slot=slot):
            for pair in range(2):
                relay_copy(pair, slot).wait_recv()
                for g in range(groups):
                    relay_on(pair, g, slot).start()


    def pass_on(pair, g):
        for slot in range(2):
            lat_arrival(pair, g, slot).wait_recv()
        for way in range(2):
            lon_copy(pair, g, way).start()

    pass_on(0, 0)
    for way in range(2):
        lon_own_copy(0, way).wait_recv()

    def query_step(g, carry):
        @pl.when(g + 1 < groups)
        def _():
            pass_on(0, g + 1)

        for c in range(groups - 1):

            @pl.when(g == c)
            def _(c=c):
                each_lat([(1, c)], start)

        query, grad = own_part(g, 2), own_part(g, 3)
        for way in range(2):
            lon_copy(0, g, way).wait_recv()
        key, value = outer_part(g, 0), outer_part(g, 1)
        query_grad = jnp.zeros((own, LANES), jnp.float32)
        stats = stat_own[...]
        for h in range(GROUP):
            grad_h = grad * in_head_half[h]
            logits = dot_nt(query * in_head_half[h], key) * to_log2 + bias[...]
            top = jnp.max(logits, axis=1, keepdims=True)
            weight = jnp.exp2(logits - top)
            total = jnp.sum(weight, axis=1, keepdims=True)
            probs = weight * (1.0 / total)
            attended = dot_nn(probs.astype(jnp.bfloat16), value)
            grad_dot = jnp.sum(grad_h.astype(jnp.float32) * attended, axis=1, keepdims=True)
            grad_probs = dot_nt(grad_h, value)
            grad_scores = (probs * (grad_probs - grad_dot)).astype(jnp.bfloat16)
            query_grad += dot_nn(grad_scores, key) * in_head[h]
            log_total = (top + jnp.log(total) * LOG2E) * (1.0 / to_log2)
            head = g * GROUP + h
            for part, stat_value in enumerate((log_total, grad_dot)):
                rest = -stat_value
                for piece in range(3):
                    kept = rest.astype(jnp.bfloat16).astype(jnp.float32)
                    rest = rest - kept
                    stats = jnp.where(lane == (3 * part + piece) * 16 + head, kept, stats)
        stat_own[...] = stats
        dq_ref[g] = (query_grad * scale).astype(jnp.bfloat16).reshape(rows, cols, LANES)
        out_copy(g, 0).start()
        return carry

    lax.fori_loop(0, groups, query_step, 0)

    stat[own_rows, pl.ds(EDGE, cols), :] = (
        stat_own[...].astype(jnp.bfloat16).reshape(rows, cols, LANES)
    )
    for way in range(2):
        stat_lat_copy(way).start()
        stat_lon_copy(0, way).start()
    each_lat([(1, groups - 1)], start)
    ahead = groups // 2
    for g in range(ahead):
        pass_on(1, g)
    for slot in range(2):
        stat_lat_arrival(slot).wait_recv()
    for way in range(2):
        stat_lon_copy(1, way).start()
    for way in range(2):
        lon_own_copy(1, way).wait_recv()

    def key_step(g, carry):
        @pl.when(g + ahead < groups)
        def _():
            pass_on(1, g + ahead)

        @pl.when(g == 0)
        def _():
            for part in range(2):
                for way in range(2):
                    stat_lon_copy(part, way).wait_recv()

        key, value = own_part(g, 0), own_part(g, 1)
        for way in range(2):
            lon_copy(1, g, way).wait_recv()
        query, grad = outer_part(g, 2), outer_part(g, 3)
        outer_stat = stat[...].reshape(outer, LANES)
        query_stat = jnp.concatenate([query, outer_stat], axis=1)
        grad_stat = jnp.concatenate([grad, outer_stat], axis=1)
        key_grad = jnp.zeros((own, LANES), jnp.float32)
        value_grad = jnp.zeros((own, LANES), jnp.float32)
        for h in range(GROUP):
            mine = lane % 16 == g * GROUP + h
            in_log = jnp.where(mine & (lane < 48), 1.0, 0.0).astype(jnp.bfloat16)
            in_dot = jnp.where(mine & (lane >= 48) & (lane < 96), 1.0, 0.0).astype(jnp.bfloat16)
            in_log = jnp.broadcast_to(in_log, (own, LANES))
            in_dot = jnp.broadcast_to(in_dot, (own, LANES))
            key_h = jnp.concatenate([key * in_head_half[h], in_log], axis=1)
            value_h = jnp.concatenate([value * in_head_half[h], in_dot], axis=1)
            probs = jnp.exp2(dot_nt(key_h, query_stat) * to_log2 + bias[...])
            value_grad += dot_nn(probs.astype(jnp.bfloat16), grad) * in_head[h]
            grad_scores = (probs * dot_nt(value_h, grad_stat)).astype(jnp.bfloat16)
            key_grad += dot_nn(grad_scores, query) * in_head[h]
        dk_ref[g] = (key_grad * scale).astype(jnp.bfloat16).reshape(rows, cols, LANES)
        out_copy(g, 1).start()
        dv_ref[g] = value_grad.astype(jnp.bfloat16).reshape(rows, cols, LANES)
        out_copy(g, 2).start()
        return carry

    lax.fori_loop(0, groups, key_step, 0)

    each_lat([(pair, g) for pair in range(2) for g in range(groups)], wait_send)
    for g in range(groups):
        for which in range(3):
            out_copy(g, which).wait()
    for way, source in enumerate((north_source, south_source)):

        @pl.when(source == 1)
        def _(way=way):
            for pair in range(2):
                relay_copy(pair, way).wait_send()

    for slot, inside in enumerate((in_north_relay, in_south_relay)):

        @pl.when(inside)
        def _(slot=slot):
            for pair in range(2):
                for g in range(groups):
                    relay_on(pair, g, slot).wait_send()

    for way in range(2):
        for pair in range(2):
            for g in range(groups):
                lon_copy(pair, g, way).wait_send()
            lon_own_copy(pair, way).wait_send()
        stat_lat_copy(way).wait_send()
        for part in range(2):
            stat_lon_copy(part, way).wait_send()


def copy_kernel(a, b, c, a_out, b_out, c_out, held, sem_in, sem_out):
    pairs = ((a, a_out), (b, b_out), (c, c_out))
    ins = [pltpu.make_async_copy(x, held.at[i], sem_in.at[i]) for i, (x, _) in enumerate(pairs)]
    outs = [pltpu.make_async_copy(held.at[i], y, sem_out.at[i]) for i, (_, y) in enumerate(pairs)]
    for copy in ins:
        copy.start()
    for copy_in, copy_out in zip(ins, outs):
        copy_in.wait()
        copy_out.start()
    for copy in outs:
        copy.wait()


def shards(n_lat, n_lon, query_field, key_field, value_field, out_grad, pole_reach):
    rows, cols, width = query_field.shape
    groups = width // LANES
    tall, wide = rows + 2 * RADIUS, cols + 2 * EDGE
    shape = jax.ShapeDtypeStruct((rows, cols, width), jnp.bfloat16)
    dma = pltpu.SemaphoreType.DMA
    results = pl.pallas_call(
        functools.partial(kernel, n_lat, n_lon, rows, cols, groups),
        out_shape=(shape, shape, shape),
        in_specs=[pl.BlockSpec(memory_space=pltpu.HBM)] * 5,
        out_specs=[pl.BlockSpec(memory_space=pltpu.HBM)] * 3,
        scratch_shapes=[
            pltpu.VMEM((groups, 4, tall, wide, LANES), jnp.bfloat16),
            pltpu.VMEM((groups, rows, cols, LANES), jnp.bfloat16),
            pltpu.VMEM((groups, rows, cols, LANES), jnp.bfloat16),
            pltpu.VMEM((groups, rows, cols, LANES), jnp.bfloat16),
            dma((3, groups)),
            pltpu.VMEM((tall, wide, LANES), jnp.bfloat16),
            pltpu.VMEM((rows * cols, LANES), jnp.float32),
            pltpu.VMEM((rows * cols, tall * wide), jnp.float32),
            pltpu.VMEM(pole_reach.shape, jnp.int32),
            dma,
            dma((groups, 4)),
            dma((2, groups, 2)),
            dma((2, groups, 2)),
            dma((2, groups, 2)),
            dma((2, groups, 2)),
            dma((2, 2)),
            dma((2, 2)),
            pltpu.VMEM((groups, 4, RADIUS, cols, LANES), jnp.bfloat16),
            dma((2,)),
            dma((2,)),
            dma((2, groups)),
            dma((2,)),
            dma((2,)),
            dma((2, 2)),
            dma((2, 2)),
        ],
        compiler_params=pltpu.CompilerParams(
            collective_id=0, has_side_effects=True, vmem_limit_bytes=60 << 20
        ),
    )(query_field, key_field, value_field, out_grad, pole_reach)
    return pl.pallas_call(
        copy_kernel,
        out_shape=(shape, shape, shape),
        in_specs=[pl.BlockSpec(memory_space=pltpu.HBM)] * 3,
        out_specs=[pl.BlockSpec(memory_space=pltpu.HBM)] * 3,
        scratch_shapes=[pltpu.VMEM((3, rows, cols, width), jnp.bfloat16), dma((3,)), dma((3,))],
        compiler_params=pltpu.CompilerParams(vmem_limit_bytes=60 << 20),
    )(*results)


def solution(mesh):
    placed = P("lat", "lon", None)
    return jax.shard_map(
        functools.partial(shards, mesh.shape["lat"], mesh.shape["lon"]),
        mesh=mesh,
        in_specs=(placed, placed, placed, placed, P()),
        out_specs=(placed, placed, placed),
        check_vma=False,
    )
```

```python
import functools
import math

import jax
import jax.numpy as jnp
from jax import lax
from jax.experimental import pallas as pl
from jax.experimental.pallas import tpu as pltpu
from jax.sharding import PartitionSpec as P

HEAD_DIM = 32
RADIUS = 6
LANES = 128
GROUP = LANES // HEAD_DIM
EDGE = 8
MESH = pl.DeviceIdType.MESH
LOG2E = 1.4426950408889634
NEG = -1e30


def dot_nt(a, b):
    return lax.dot_general(a, b, (((1,), (1,)), ((), ())), preferred_element_type=jnp.float32)


def dot_nn(a, b):
    return lax.dot_general(a, b, (((1,), (0,)), ((), ())), preferred_element_type=jnp.float32)


def kernel(
    n_lat,
    n_lon,
    rows,
    cols,
    groups,
    q_ref,
    k_ref,
    v_ref,
    g_ref,
    reach_hbm,
    dq_hbm,
    dk_hbm,
    dv_hbm,
    field,
    dq_ref,
    dk_ref,
    dv_ref,
    out_sem,
    stat,
    stat_own,
    bias,
    reach_ref,
    reach_sem,
    local_sem,
    lat_send,
    lat_recv,
    lon_send,
    lon_recv,
    lon_own_send,
    lon_own_recv,
    relayed,
    relay_send,
    relay_recv,
    relay_on_send,
    stat_lat_send,
    stat_lat_recv,
    stat_lon_send,
    stat_lon_recv,
):
    lat, lon = lax.axis_index("lat"), lax.axis_index("lon")
    tall, wide = rows + 2 * RADIUS, cols + 2 * EDGE
    own, outer = rows * cols, tall * wide
    own_rows, halo_rows = pl.ds(0, rows), pl.ds(rows, 2 * RADIUS)
    at_north = (n_lat - 1 - lat) // (n_lat - 1)
    at_south = lat // (n_lat - 1)
    up = (lat - 1 + at_north, (lon + at_north * (n_lon // 2)) % n_lon)
    down = (lat + 1 - at_south, (lon + at_south * (n_lon // 2)) % n_lon)
    up_slot, down_slot = 1 - at_north, at_south
    left = (lat, (lon + n_lon - 1) % n_lon)
    right = (lat, (lon + 1) % n_lon)

    sources = (k_ref, v_ref, q_ref, g_ref)

    def local_copy(g, a):
        return pltpu.make_async_copy(
            sources[a].at[:, :, pl.ds(g * LANES, LANES)],
            field.at[g, a, own_rows, pl.ds(EDGE, cols), :],
            local_sem.at[g, a],
        )

    for pair in range(2):
        for g in range(groups):
            for a in range(2):
                local_copy(g, 2 * pair + a).start()

    reach_copy = pltpu.make_async_copy(reach_hbm, reach_ref, reach_sem)
    reach_copy.start()

    half_lon = n_lon // 2
    half = lon // half_lon
    north_relay, south_relay = n_lat - 4, 3
    north_source, south_source = at_north * (1 - half), at_south * half
    in_north_relay = (lat == north_relay) & (half == 0)
    in_south_relay = (lat == south_relay) & (half == 1)
    relay = (
        at_north * north_relay + at_south * south_relay,
        lon % half_lon + at_south * half_lon,
    )
    relay_ends = (
        ((0, lon), (0, (lon + half_lon) % n_lon)),
        ((n_lat - 1, lon), (n_lat - 1, (lon + half_lon) % n_lon)),
    )

    for edge in (pl.ds(0, EDGE), pl.ds(EDGE + cols, EDGE)):
        field[:, :, :, edge, :] = jnp.zeros((groups, 4, tall, EDGE, LANES), jnp.bfloat16)
        stat[:, edge, :] = jnp.zeros((tall, EDGE, LANES), jnp.bfloat16)

    barrier = pltpu.get_barrier_semaphore()

    def greet(device):
        pl.semaphore_signal(barrier, inc=1, device_id=device, device_id_type=MESH)

    for device in (up, down, left, right):
        greet(device)

    @pl.when(at_north + at_south == 1)
    def _():
        greet(relay)

    for inside, ends in zip((in_north_relay, in_south_relay), relay_ends):

        @pl.when(inside)
        def _(ends=ends):
            for device in ends:
                greet(device)

    def relay_copy(pair, way):
        arrays = pl.ds(2 * pair, 2)
        return pltpu.make_async_remote_copy(
            src_ref=field.at[:, arrays, pl.ds((0, rows - RADIUS)[way], RADIUS), pl.ds(EDGE, cols), :],
            dst_ref=relayed.at[:, arrays],
            send_sem=relay_send.at[pair],
            recv_sem=relay_recv.at[pair],
            device_id=relay,
            device_id_type=MESH,
        )

    def relay_on(pair, g, slot):
        arrays = pl.ds(2 * pair, 2)
        return pltpu.make_async_remote_copy(
            src_ref=relayed.at[g, arrays],
            dst_ref=field.at[g, arrays, pl.ds(rows + slot * RADIUS, RADIUS), pl.ds(EDGE, cols), :],
            send_sem=relay_on_send.at[pair, g],
            recv_sem=lat_recv.at[pair, g, slot],
            device_id=relay_ends[slot][1],
            device_id_type=MESH,
        )

    def lat_copy(pair, g, way):
        arrays = pl.ds(2 * pair, 2)
        slot = (up_slot, down_slot)[way]
        return pltpu.make_async_remote_copy(
            src_ref=field.at[g, arrays, pl.ds((0, rows - RADIUS)[way], RADIUS), pl.ds(EDGE, cols), :],
            dst_ref=field.at[g, arrays, pl.ds(rows + slot * RADIUS, RADIUS), pl.ds(EDGE, cols), :],
            send_sem=lat_send.at[pair, g, way],
            recv_sem=lat_recv.at[pair, g, slot],
            device_id=(up, down)[way],
            device_id_type=MESH,
        )

    def lat_arrival(pair, g, slot):
        arrays = pl.ds(2 * pair, 2)
        there = field.at[g, arrays, pl.ds(rows + slot * RADIUS, RADIUS), pl.ds(EDGE, cols), :]
        return pltpu.make_async_remote_copy(
            src_ref=there,
            dst_ref=there,
            send_sem=lat_send.at[pair, g, slot],
            recv_sem=lat_recv.at[pair, g, slot],
            device_id=up,
            device_id_type=MESH,
        )

    def lon_copy(pair, g, way):
        arrays = pl.ds(2 * pair, 2)
        return pltpu.make_async_remote_copy(
            src_ref=field.at[g, arrays, halo_rows, pl.ds((EDGE, EDGE + cols - RADIUS)[way], RADIUS), :],
            dst_ref=field.at[g, arrays, halo_rows, pl.ds((EDGE + cols, EDGE - RADIUS)[way], RADIUS), :],
            send_sem=lon_send.at[pair, g, way],
            recv_sem=lon_recv.at[pair, g, way],
            device_id=(left, right)[way],
            device_id_type=MESH,
        )

    def lon_own_copy(pair, way):
        arrays = pl.ds(2 * pair, 2)
        return pltpu.make_async_remote_copy(
            src_ref=field.at[:, arrays, own_rows, pl.ds((EDGE, EDGE + cols - RADIUS)[way], RADIUS), :],
            dst_ref=field.at[:, arrays, own_rows, pl.ds((EDGE + cols, EDGE - RADIUS)[way], RADIUS), :],
            send_sem=lon_own_send.at[pair, way],
            recv_sem=lon_own_recv.at[pair, way],
            device_id=(left, right)[way],
            device_id_type=MESH,
        )

    def stat_lat_copy(way):
        slot = (up_slot, down_slot)[way]
        return pltpu.make_async_remote_copy(
            src_ref=stat.at[pl.ds((0, rows - RADIUS)[way], RADIUS), pl.ds(EDGE, cols), :],
            dst_ref=stat.at[pl.ds(rows + slot * RADIUS, RADIUS), pl.ds(EDGE, cols), :],
            send_sem=stat_lat_send.at[way],
            recv_sem=stat_lat_recv.at[slot],
            device_id=(up, down)[way],
            device_id_type=MESH,
        )

    def stat_lat_arrival(slot):
        there = stat.at[pl.ds(rows + slot * RADIUS, RADIUS), pl.ds(EDGE, cols), :]
        return pltpu.make_async_remote_copy(
            src_ref=there,
            dst_ref=there,
            send_sem=stat_lat_send.at[slot],
            recv_sem=stat_lat_recv.at[slot],
            device_id=up,
            device_id_type=MESH,
        )

    def stat_lon_copy(part, way):
        span = (own_rows, halo_rows)[part]
        return pltpu.make_async_remote_copy(
            src_ref=stat.at[span, pl.ds((EDGE, EDGE + cols - RADIUS)[way], RADIUS), :],
            dst_ref=stat.at[span, pl.ds((EDGE + cols, EDGE - RADIUS)[way], RADIUS), :],
            send_sem=stat_lon_send.at[part, way],
            recv_sem=stat_lon_recv.at[part, way],
            device_id=(left, right)[way],
            device_id_type=MESH,
        )

    def each_lat(chunks, act):
        for skipped, ways in ((north_source, (1,)), (south_source, (0,)), (None, (0, 1))):
            here = north_source + south_source == 0 if skipped is None else skipped == 1

            @pl.when(here)
            def _(ways=ways):
                for pair, g in chunks:
                    for way in ways:
                        act(lat_copy(pair, g, way))

    def start(copy):
        copy.start()

    def wait_send(copy):
        copy.wait_send()

    for g in range(groups):
        for a in range(4):
            local_copy(g, a).wait()
    polar, relaying = at_north + at_south == 1, in_north_relay | in_south_relay
    for here, peers in (
        (polar, 5),
        (relaying, 6),
        (jnp.logical_not(polar | relaying), 4),
    ):

        @pl.when(here)
        def _(peers=peers):
            pl.semaphore_wait(barrier, peers)

    for way, source in enumerate((north_source, south_source)):

        @pl.when(source == 1)
        def _(way=way):
            for pair in range(2):
                relay_copy(pair, way).start()

    for way in range(2):
        lon_own_copy(0, way).start()
    each_lat([(0, g) for g in range(groups)], start)
    for way in range(2):
        lon_own_copy(1, way).start()
    reach_copy.wait()

    total_cols = n_lon * cols
    reach = reach_ref[...].astype(jnp.float32)
    pick = lax.broadcasted_iota(jnp.int32, (16, total_cols), 0)
    table = jnp.where(
        pick == 0,
        jnp.broadcast_to(reach[0:1], (16, total_cols)),
        jnp.where(pick == 1, jnp.broadcast_to(reach[1:2], (16, total_cols)), 0.0),
    ).astype(jnp.bfloat16)
    outer_at = lax.broadcasted_iota(jnp.int32, (total_cols, outer), 1)
    outer_col = (lon * cols + outer_at % wide + (total_cols - EDGE + total_cols // 2)) % total_cols
    hit = lax.broadcasted_iota(jnp.int32, (total_cols, outer), 0) == outer_col
    key_reach = dot_nn(table, jnp.where(hit, 1.0, 0.0).astype(jnp.bfloat16))
    own_at = lax.broadcasted_iota(jnp.int32, (own, total_cols), 0)
    hit = lax.broadcasted_iota(jnp.int32, (own, total_cols), 1) == lon * cols + own_at % cols
    query_reach = dot_nt(jnp.where(hit, 1.0, 0.0).astype(jnp.bfloat16), table)
    k_at = lax.broadcasted_iota(jnp.int32, (1, outer), 1)
    k_row, k_col = k_at // wide, k_at % wide - EDGE
    k_above, k_below = k_row - rows, k_row - rows - RADIUS
    k_north = (k_above >= 0) & (k_below < 0) & (at_north == 1)
    k_south = (k_below >= 0) & (at_south == 1)
    k_place = jnp.where(
        k_below >= 0,
        jnp.where(k_south, rows + RADIUS - 1 - k_below, rows + k_below),
        jnp.where(k_above >= 0, jnp.where(k_north, -1 - k_above, k_above - RADIUS), k_row),
    )
    k_depth = jnp.where(k_north, k_above, RADIUS - 1 - k_below).astype(jnp.float32)
    k_polar = jnp.where(k_north, 1.0, jnp.where(k_south, 2.0, 0.0))
    k_ok = jnp.where(
        k_north,
        jnp.where(key_reach[0:1] > k_depth, 1.0, 0.0),
        jnp.where(k_south, jnp.where(key_reach[1:2] > k_depth, 1.0, 0.0), 1.0),
    )
    q_at = lax.broadcasted_iota(jnp.int32, (own, 1), 0)
    q_row, q_col = q_at // cols, q_at % cols
    q_north = jnp.where(query_reach[:, 0:1] > q_row.astype(jnp.float32), 1.0, 0.0)
    q_south = jnp.where(query_reach[:, 1:2] > (rows - 1 - q_row).astype(jnp.float32), 1.0, 0.0)
    near = (jnp.abs(k_place - q_row) <= RADIUS) & (jnp.abs(k_col - q_col) <= RADIUS)
    q_ok = jnp.where(k_polar == 1.0, q_north, jnp.where(k_polar == 2.0, q_south, 1.0))
    bias[...] = jnp.where(near & (q_ok * k_ok > 0.5), 0.0, NEG)

    lane = lax.broadcasted_iota(jnp.int32, (1, LANES), 1)
    in_head = [jnp.where(lane // HEAD_DIM == h, 1.0, 0.0) for h in range(GROUP)]
    in_head_half = [mask.astype(jnp.bfloat16) for mask in in_head]
    scale = 1.0 / math.sqrt(HEAD_DIM)
    to_log2 = scale * LOG2E

    def own_part(g, a):
        return field[g, a, own_rows, pl.ds(EDGE, cols), :].reshape(own, LANES)

    def outer_part(g, a):
        return field[g, a].reshape(outer, LANES)

    def features(g):
        return pl.ds(pl.multiple_of(g * LANES, LANES), LANES)

    results = ((dq_ref, dq_hbm), (dk_ref, dk_hbm), (dv_ref, dv_hbm))

    def out_copy(g, which):
        held, result = results[which]
        return pltpu.make_async_copy(
            held.at[g], result.at[:, :, features(g)], out_sem.at[which, g]
        )

    stat_own[...] = jnp.zeros_like(stat_own)

    for slot, inside in enumerate((in_north_relay, in_south_relay)):

        @pl.when(inside)
        def _(slot=slot):
            for pair in range(2):
                relay_copy(pair, slot).wait_recv()
                for g in range(groups):
                    relay_on(pair, g, slot).start()


    def pass_on(pair, g):
        for slot in range(2):
            lat_arrival(pair, g, slot).wait_recv()
        for way in range(2):
            lon_copy(pair, g, way).start()

    pass_on(0, 0)
    for way in range(2):
        lon_own_copy(0, way).wait_recv()

    def query_step(g, carry):
        @pl.when(g + 1 < groups)
        def _():
            pass_on(0, g + 1)

        for c in range(groups - 1):

            @pl.when(g == c)
            def _(c=c):
                each_lat([(1, c)], start)

        query, grad = own_part(g, 2), own_part(g, 3)
        for way in range(2):
            lon_copy(0, g, way).wait_recv()
        key, value = outer_part(g, 0), outer_part(g, 1)
        query_grad = jnp.zeros((own, LANES), jnp.float32)
        stats = stat_own[...]
        for h in range(0, GROUP, 2):
            grad_h = jnp.concatenate([grad * in_head_half[h], grad * in_head_half[h + 1]], axis=0)
            query_h = jnp.concatenate(
                [query * in_head_half[h], query * in_head_half[h + 1]], axis=0
            )
            logits = (dot_nt(query_h, key) * to_log2).reshape(2, own, outer) + bias[...][None]
            logits = logits.reshape(2 * own, outer)
            top = jnp.max(logits, axis=1, keepdims=True)
            weight = jnp.exp2(logits - top)
            total = jnp.sum(weight, axis=1, keepdims=True)
            probs = weight * (1.0 / total)
            attended = dot_nn(probs.astype(jnp.bfloat16), value)
            grad_dot = jnp.sum(grad_h.astype(jnp.float32) * attended, axis=1, keepdims=True)
            grad_probs = dot_nt(grad_h, value)
            grad_scores = (probs * (grad_probs - grad_dot)).astype(jnp.bfloat16)
            both = dot_nn(grad_scores, key)
            query_grad += both[:own] * in_head[h] + both[own:] * in_head[h + 1]
            log_total = (top + jnp.log(total) * LOG2E) * (1.0 / to_log2)
            for part, stat_value in enumerate((log_total, grad_dot)):
                rest = -stat_value
                for piece in range(3):
                    kept = rest.astype(jnp.bfloat16).astype(jnp.float32)
                    rest = rest - kept
                    for i in range(2):
                        at = lane == (3 * part + piece) * 16 + g * GROUP + h + i
                        stats = jnp.where(at, kept[i * own : (i + 1) * own], stats)
        stat_own[...] = stats
        dq_ref[g] = (query_grad * scale).astype(jnp.bfloat16).reshape(rows, cols, LANES)
        out_copy(g, 0).start()
        return carry

    lax.fori_loop(0, groups, query_step, 0)

    stat[own_rows, pl.ds(EDGE, cols), :] = (
        stat_own[...].astype(jnp.bfloat16).reshape(rows, cols, LANES)
    )
    for way in range(2):
        stat_lat_copy(way).start()
        stat_lon_copy(0, way).start()
    each_lat([(1, groups - 1)], start)
    ahead = groups // 2
    for g in range(ahead):
        pass_on(1, g)
    for slot in range(2):
        stat_lat_arrival(slot).wait_recv()
    for way in range(2):
        stat_lon_copy(1, way).start()
    for way in range(2):
        lon_own_copy(1, way).wait_recv()

    def key_step(g, carry):
        @pl.when(g + ahead < groups)
        def _():
            pass_on(1, g + ahead)

        @pl.when(g == 0)
        def _():
            for part in range(2):
                for way in range(2):
                    stat_lon_copy(part, way).wait_recv()

        key, value = own_part(g, 0), own_part(g, 1)
        for way in range(2):
            lon_copy(1, g, way).wait_recv()
        query, grad = outer_part(g, 2), outer_part(g, 3)
        outer_stat = stat[...].reshape(outer, LANES)
        query_stat = jnp.concatenate([query, outer_stat], axis=1)
        grad_stat = jnp.concatenate([grad, outer_stat], axis=1)
        key_grad = jnp.zeros((own, LANES), jnp.float32)
        value_grad = jnp.zeros((own, LANES), jnp.float32)
        for h in range(0, GROUP, 2):
            keys, values = [], []
            for i in range(2):
                mine = lane % 16 == g * GROUP + h + i
                in_log = jnp.where(mine & (lane < 48), 1.0, 0.0).astype(jnp.bfloat16)
                in_dot = jnp.where(mine & (lane >= 48) & (lane < 96), 1.0, 0.0).astype(jnp.bfloat16)
                in_log = jnp.broadcast_to(in_log, (own, LANES))
                in_dot = jnp.broadcast_to(in_dot, (own, LANES))
                keys.append(jnp.concatenate([key * in_head_half[h + i], in_log], axis=1))
                values.append(jnp.concatenate([value * in_head_half[h + i], in_dot], axis=1))
            key_h, value_h = jnp.concatenate(keys, axis=0), jnp.concatenate(values, axis=0)
            logits = (dot_nt(key_h, query_stat) * to_log2).reshape(2, own, outer) + bias[...][None]
            probs = jnp.exp2(logits.reshape(2 * own, outer))
            both = dot_nn(probs.astype(jnp.bfloat16), grad)
            value_grad += both[:own] * in_head[h] + both[own:] * in_head[h + 1]
            grad_scores = (probs * dot_nt(value_h, grad_stat)).astype(jnp.bfloat16)
            both = dot_nn(grad_scores, query)
            key_grad += both[:own] * in_head[h] + both[own:] * in_head[h + 1]
        dk_ref[g] = (key_grad * scale).astype(jnp.bfloat16).reshape(rows, cols, LANES)
        out_copy(g, 1).start()
        dv_ref[g] = value_grad.astype(jnp.bfloat16).reshape(rows, cols, LANES)
        out_copy(g, 2).start()
        return carry

    lax.fori_loop(0, groups, key_step, 0)

    each_lat([(pair, g) for pair in range(2) for g in range(groups)], wait_send)
    for g in range(groups):
        for which in range(3):
            out_copy(g, which).wait()
    for way, source in enumerate((north_source, south_source)):

        @pl.when(source == 1)
        def _(way=way):
            for pair in range(2):
                relay_copy(pair, way).wait_send()

    for slot, inside in enumerate((in_north_relay, in_south_relay)):

        @pl.when(inside)
        def _(slot=slot):
            for pair in range(2):
                for g in range(groups):
                    relay_on(pair, g, slot).wait_send()

    for way in range(2):
        for pair in range(2):
            for g in range(groups):
                lon_copy(pair, g, way).wait_send()
            lon_own_copy(pair, way).wait_send()
        stat_lat_copy(way).wait_send()
        for part in range(2):
            stat_lon_copy(part, way).wait_send()


def copy_kernel(a, b, c, a_out, b_out, c_out, held, sem_in, sem_out):
    pairs = ((a, a_out), (b, b_out), (c, c_out))
    ins = [pltpu.make_async_copy(x, held.at[i], sem_in.at[i]) for i, (x, _) in enumerate(pairs)]
    outs = [pltpu.make_async_copy(held.at[i], y, sem_out.at[i]) for i, (_, y) in enumerate(pairs)]
    for copy in ins:
        copy.start()
    for copy_in, copy_out in zip(ins, outs):
        copy_in.wait()
        copy_out.start()
    for copy in outs:
        copy.wait()


def shards(n_lat, n_lon, query_field, key_field, value_field, out_grad, pole_reach):
    rows, cols, width = query_field.shape
    groups = width // LANES
    tall, wide = rows + 2 * RADIUS, cols + 2 * EDGE
    shape = jax.ShapeDtypeStruct((rows, cols, width), jnp.bfloat16)
    dma = pltpu.SemaphoreType.DMA
    results = pl.pallas_call(
        functools.partial(kernel, n_lat, n_lon, rows, cols, groups),
        out_shape=(shape, shape, shape),
        in_specs=[pl.BlockSpec(memory_space=pltpu.HBM)] * 5,
        out_specs=[pl.BlockSpec(memory_space=pltpu.HBM)] * 3,
        scratch_shapes=[
            pltpu.VMEM((groups, 4, tall, wide, LANES), jnp.bfloat16),
            pltpu.VMEM((groups, rows, cols, LANES), jnp.bfloat16),
            pltpu.VMEM((groups, rows, cols, LANES), jnp.bfloat16),
            pltpu.VMEM((groups, rows, cols, LANES), jnp.bfloat16),
            dma((3, groups)),
            pltpu.VMEM((tall, wide, LANES), jnp.bfloat16),
            pltpu.VMEM((rows * cols, LANES), jnp.float32),
            pltpu.VMEM((rows * cols, tall * wide), jnp.float32),
            pltpu.VMEM(pole_reach.shape, jnp.int32),
            dma,
            dma((groups, 4)),
            dma((2, groups, 2)),
            dma((2, groups, 2)),
            dma((2, groups, 2)),
            dma((2, groups, 2)),
            dma((2, 2)),
            dma((2, 2)),
            pltpu.VMEM((groups, 4, RADIUS, cols, LANES), jnp.bfloat16),
            dma((2,)),
            dma((2,)),
            dma((2, groups)),
            dma((2,)),
            dma((2,)),
            dma((2, 2)),
            dma((2, 2)),
        ],
        compiler_params=pltpu.CompilerParams(
            collective_id=0, has_side_effects=True, vmem_limit_bytes=60 << 20
        ),
    )(query_field, key_field, value_field, out_grad, pole_reach)
    return pl.pallas_call(
        copy_kernel,
        out_shape=(shape, shape, shape),
        in_specs=[pl.BlockSpec(memory_space=pltpu.HBM)] * 3,
        out_specs=[pl.BlockSpec(memory_space=pltpu.HBM)] * 3,
        scratch_shapes=[pltpu.VMEM((3, rows, cols, width), jnp.bfloat16), dma((3,)), dma((3,))],
        compiler_params=pltpu.CompilerParams(vmem_limit_bytes=60 << 20),
    )(*results)


def solution(mesh):
    placed = P("lat", "lon", None)
    return jax.shard_map(
        functools.partial(shards, mesh.shape["lat"], mesh.shape["lon"]),
        mesh=mesh,
        in_specs=(placed, placed, placed, placed, P()),
        out_specs=(placed, placed, placed),
        check_vma=False,
    )
```
